32 devices in a mesh: mode: 4 (over y, x), rest: 8 (over z, core).
Axes of the slice: x: 2, y: 2, z: 4, core: 2. Of those that a mesh axis runs over, the one named last changes fastest.
Arguments:
- unfolded: float32 [512, 65536], P('mode', 'rest'), may hold values from -150 to 150
- start_block: float32 [512, 128], replicated, may hold values from -6 to 6
Outputs:
- triangle: float32 [512, 512], replicated
- factor: float32 [512, 128], replicated
- core: float32 [128, 65536], P('mode', 'rest')
The draws below stay inside these ranges and needn't reach their ends.
All inputs are finite; a program needn't handle non-finite values.
Results may differ from the reference program's by a relative error of at most 0.0003.
Values sent between devices are 32-bit elements; how exact they have to be, the bound alone decides.
A program may use at most 64 MiB of HBM per device.

```python
import math
import jax
import jax.numpy as jnp
from jax import lax

M = 512
R = 128
ITERS = 3
COLS = 65536


def draw_unfolded(key, part):
    keys = jax.random.split(jax.random.fold_in(key, 11), 4)
    noise = jax.random.truncated_normal(keys[0], -5.0, 5.0, (M, COLS), jnp.float32)
    col_low = math.log(0.7)
    col_high = math.log(1.4)
    mixing = jnp.eye(M, dtype=jnp.float32) + 0.03 * jax.random.normal(keys[1], (M, M), jnp.float32)
    row_scale = jnp.exp(jax.random.uniform(keys[2], (M,), jnp.float32, 0.0, math.log(4.0)))
    position = jnp.arange(COLS, dtype=jnp.float32) / COLS
    col_scale = (1.0 + 2.0 * position) * jnp.exp(jax.random.uniform(keys[3], (COLS,), jnp.float32, col_low, col_high))
    mixed = jnp.dot(mixing, noise, precision=lax.Precision.HIGHEST)
    return row_scale[:, None] * mixed * col_scale[None, :]


def gaussian(stream_key, extent, width, reach, kind=jnp.bfloat16):
    values = width * jax.random.normal(stream_key, extent, jnp.float32)
    return jnp.clip(values, min=-reach, max=reach).astype(kind)


def setup_inputs(seed: int = 0) -> dict:
    key_list = jax.random.split(jax.random.key(seed), 3)
    unfolded = draw_unfolded(jax.random.fold_in(key_list[2], 71), 0)
    start_block = gaussian(key_list[1], (M, R), 1.0, 6.0, jnp.float32)
    return dict(unfolded=unfolded, start_block=start_block)


def orthogonal_steps(triangle, start_block):
    highest = lax.Precision.HIGHEST
    columns_now = start_block
    for repeat in range(ITERS):
        inner = jnp.dot(triangle.T, columns_now, precision=highest)
        image = jnp.dot(triangle, inner, precision=highest)
        projected = jnp.dot(image.T, image, precision=highest)
        small_factor = jnp.linalg.cholesky(projected)
        columns_now = lax.linalg.triangular_solve(small_factor, image, left_side=False, lower=True, transpose_a=True)
    return columns_now

def reference(unfolded, start_block):
    highest = lax.Precision.HIGHEST
    gram = jnp.dot(unfolded, unfolded.T, precision=highest) / COLS
    triangle = jnp.linalg.cholesky(gram)
    factor = orthogonal_steps(triangle, start_block)
    core = jnp.dot(factor.T, unfolded, precision=highest)
    return (triangle, factor, core)
```

```python
import functools

import jax
import jax.numpy as jnp
from jax import lax
from jax.experimental import pallas as pl
from jax.experimental.pallas import tpu as pltpu
from jax.sharding import PartitionSpec as P

ITERS = 3
SUB = 8
STEP = 16
SLICES = 2
LATE = 2
LANES = 128
F32 = jnp.float32
BF16 = jnp.bfloat16
MESH = pl.DeviceIdType.MESH


def parts3(x):
    hi = x.astype(BF16).astype(F32)
    rest = x - hi
    mid = rest.astype(BF16).astype(F32)
    return hi, mid, rest - mid


def nt(x, y):
    return lax.dot_general(x, y, (((1,), (1,)), ((), ())), preferred_element_type=F32)


def nn(x, y):
    return lax.dot_general(x, y, (((1,), (0,)), ((), ())), preferred_element_type=F32)


def dotf(x, y, dims):
    return lax.dot_general(
        x, y, (dims, ((), ())), precision=lax.Precision.HIGHEST, preferred_element_type=F32
    )


def eliminate(ref, row, col, width, block):
    r0 = pl.multiple_of(block * STEP, STEP)
    chunks = [ref[pl.ds(row + r0, STEP), pl.ds(col + c, LANES)] for c in range(0, width, LANES)]
    sub = lax.broadcasted_iota(jnp.int32, (STEP, LANES), 0)
    cols = [
        jnp.take_along_axis(chunks[0], jnp.full((STEP, LANES), r0 + k, jnp.int32), axis=1) for k in range(STEP)
    ]
    pivots = jnp.ones((STEP, LANES), F32)
    for k in range(STEP):
        p = cols[k][k : k + 1, :]
        f = jnp.where(sub > k, cols[k] * (1.0 / p), 0.0)
        pivots = jnp.where(sub == k, p, pivots)
        for j in range(k + 1, STEP):
            cols[j] = cols[j] - f * cols[j][k : k + 1, :]
        chunks = [v - f * v[k : k + 1, :] for v in chunks]
    s = lax.rsqrt(pivots)
    s = s * (1.5 - 0.5 * pivots * s * s)
    chunks = [v * s for v in chunks]
    v = jnp.concatenate(chunks, axis=1)
    ref[pl.ds(row + r0, STEP), pl.ds(col, width)] = v
    lane = lax.broadcasted_iota(jnp.int32, (STEP, LANES), 1)
    keep = lane >= r0 + STEP
    hi, mid, lo = parts3(v)
    lh, lm, ll = (jnp.where(keep, x[:, :LANES], 0.0) for x in (hi, mid, lo))
    left = jnp.concatenate([lh, lh, lm, lm, lh, ll], axis=0).astype(BF16)
    right = jnp.concatenate([hi, mid, hi, mid, lo, hi], axis=0).astype(BF16)
    upd = lax.dot_general(left, right, (((0,), (0,)), ((), ())), preferred_element_type=F32)
    ref[pl.ds(row, LANES), pl.ds(col, width)] -= upd


def block_pairs(count):
    return [(i, j) for i in range(count) for j in range(i, count)]


def cuts(width, weights):
    unit = width // sum(weights)
    starts = [unit * sum(weights[:k]) for k in range(len(weights))]
    return [(start, unit * weight) for start, weight in zip(starts, weights)]


def split(x):
    hi = x.astype(BF16)
    return hi, (x - hi.astype(F32)).astype(BF16)


def off_pairs(count):
    return [(i, j) for i in range(count) for j in range(i + 1, count)]


def owners_of(depth):
    return (depth // 4, depth // 2) if depth % 4 == 0 else (0, depth)


GATHER = (3, 2, 2, 1)
SCATTER = (1, 1, 2, 2, 2)


def kernel(shape, total_cols, x_ref, start_ref, tri_ref, factor_ref, core_ref,
           full, hi_ref, lo_ref, own, part, acc, tot, dacc, dtot, got_c, got_m, got_z, sum1, sum2, dgot_c, dgot_z,
           work, gram_ref, aug, begin,
           row_s, row_r, row_l, own_l, c_s, c_r, m_s, m_r, z_s, z_r, az_s, az_r, am_s, am_r, ac_s, ac_r,
           dc_s, dc_r, dz_s, dz_r, dm_s, dm_r, df_s, df_r, out_s, out_r):
    modes, cores, depth = shape
    me_mode = lax.axis_index("mode")
    me_rest = lax.axis_index("rest")
    me_core = lax.rem(me_rest, cores)
    me_z = me_rest // cores
    first_owner, owners = owners_of(depth)
    is_owner = jnp.logical_and(me_z >= first_owner, me_z < first_owner + owners)
    m, width = full.shape
    rows_dev, cols_dev = x_ref.shape
    rounds = m // LANES

    def mode_peer(off):
        other = lax.rem(me_mode + off, modes)
        return other, (other, me_rest)

    def core_peer(off):
        other = lax.rem(me_core + off, cores)
        return other, (me_mode, me_z * cores + other)

    def z_peer(off):
        other = lax.rem(me_z + off, depth)
        return other, (me_mode, other * cores + me_core)

    def remote(source, target, send, recv, device):
        return pltpu.make_async_remote_copy(
            src_ref=source, dst_ref=target, send_sem=send, recv_sem=recv, device_id=device, device_id_type=MESH
        )

    def at(start, size):
        return pl.ds(pl.multiple_of(start, SUB), size)

    def each_z(body):
        def step(off, carry):
            body(off)
            return carry
        lax.fori_loop(1, depth, step, 0)

    barrier = pltpu.get_barrier_semaphore()
    for peer, size in ((core_peer, cores), (mode_peer, modes)):
        for off in range(1, size):
            pl.semaphore_signal(barrier, inc=1, device_id=peer(off)[1], device_id_type=MESH)
    each_z(lambda off: pl.semaphore_signal(barrier, inc=1, device_id=z_peer(off)[1], device_id_type=MESH))
    pl.semaphore_wait(barrier, modes + cores + depth - 3)

    pieces = cuts(width, GATHER)
    mine_rows = pl.ds(pl.multiple_of(me_mode * rows_dev, rows_dev), rows_dev)
    arrivals = []
    for c, (start, size) in enumerate(pieces):
        spot = (mine_rows, pl.ds(start, size))
        batch = []
        for off in range(1, modes):
            other, device = mode_peer(off)
            batch.append(remote(
                x_ref.at[:, pl.ds(pl.multiple_of(other * width + start, LANES), size)], full.at[spot],
                row_s.at[c, off], row_r.at[c, off], device,
            ))
        batch.append(pltpu.make_async_copy(
            x_ref.at[:, pl.ds(pl.multiple_of(me_mode * width + start, LANES), size)], full.at[spot], row_l.at[c]
        ))
        for copy in batch:
            copy.start()
        arrivals.append(batch)
    loads = []
    for q in range(modes):
        cols = pl.ds(q * width, width)
        load = pltpu.make_async_copy(x_ref.at[:, cols], own.at[:, cols], own_l.at[q])
        load.start()
        loads.append(load)

    fetch = pltpu.make_async_copy(start_ref, begin, own_l.at[modes])
    fetch.start()
    dacc[...] = jnp.zeros_like(dacc)
    acc[...] = jnp.zeros_like(acc)
    for q in range(modes):
        loads[q].wait()
        h, l = split(own[:, pl.ds(q * width, width)])
        cross = nt(h, l)
        dacc[...] += nt(h, h) + (cross + cross.T)
    half = rows_dev // cores
    pending = []
    for off in range(1, cores):
        other, device = core_peer(off)
        copy = remote(dacc.at[at(other * half, half)], dgot_c.at[off - 1], dc_s.at[off], dc_r.at[off], device)
        copy.start()
        pending.append(copy)

    pairs = off_pairs(rounds)

    def absorb(c):
        for copy in arrivals[c]:
            copy.wait()
        start, size = pieces[c]
        cols = pl.ds(start, size)
        hi, lo = split(full[:, cols])
        hi_ref[:, cols] = hi
        lo_ref[:, cols] = lo
        for i in range(rounds - 1):
            top = slice(i * LANES, (i + 1) * LANES)
            rest = slice((i + 1) * LANES, m)
            strip = nt(hi[top], hi[rest]) + (nt(hi[top], lo[rest]) + nt(lo[top], hi[rest]))
            for j in range(i + 1, rounds):
                spot = pl.ds(pairs.index((i, j)) * LANES, LANES)
                acc[spot, :] += strip[:, (j - i - 1) * LANES : (j - i) * LANES]

    absorb(0)
    fetch.wait()
    for copy in pending:
        copy.wait()
    value = dacc[at(me_core * half, half), :]
    for off in range(1, cores):
        value = value + dgot_c[off - 1]
    dgot_z[me_z] = value

    def dz_copy(off):
        _, device = z_peer(off)
        return remote(dgot_z.at[me_z], dgot_z.at[me_z], dz_s.at[off], dz_r.at[off], device)

    each_z(lambda off: dz_copy(off).start())
    absorb(1)
    each_z(lambda off: dz_copy(off).wait())
    value = lax.fori_loop(1, depth, lambda z, v: v + dgot_z[z], dgot_z[0])
    dmine = at(me_mode * rows_dev + me_core * half, half)
    dtot[dmine, :] = value / total_cols
    for c in range(2, len(pieces)):
        absorb(c)

    padded = acc.shape[0]
    h0 = padded // SLICES
    h1 = h0 // cores
    h2 = h1 // modes
    h3 = h2 // owners
    sends = []

    stage_c = []
    for s in range(SLICES):
        batch = []
        for off in range(1, cores):
            other, device = core_peer(off)
            copy = remote(acc.at[at(s * h0 + other * h1, h1)], got_c.at[s, off - 1], c_s.at[s, off], c_r.at[s, off], device)
            copy.start()
            batch.append(copy)
        stage_c.append(batch)
    stage_m = []
    for s in range(SLICES):
        value = acc[at(s * h0 + me_core * h1, h1), :]
        for off, copy in enumerate(stage_c[s]):
            copy.wait_recv()
            value = value + got_c[s, off]
        sends += stage_c[s]
        sum1[s] = value
        batch = []
        for off in range(1, modes):
            other, device = mode_peer(off)
            copy = remote(sum1.at[s, at(other * h2, h2)], got_m.at[s, off - 1], m_s.at[s, off], m_r.at[s, off], device)
            copy.start()
            batch.append(copy)
        stage_m.append(batch)
    stage_d = []
    for off in range(1, modes):
        other, device = mode_peer(off)
        copy = remote(dtot.at[dmine], dtot.at[dmine], dm_s.at[off], dm_r.at[off], device)
        copy.start()
        stage_d.append(copy)

    def forward(ref, spot, send, recv):
        for off in range(1, cores):
            _, device = core_peer(off)
            copy = remote(ref.at[spot], ref.at[spot], send.at[off], recv.at[off], device)
            copy.start()
            sends.append(copy)
            relays.append(copy)

    relays = []
    forward(dtot, dmine, df_s.at[0], df_r.at[0])

    def z_copy(s, off):
        other, device = z_peer(off)
        return remote(
            sum2.at[s, at(jnp.clip(other - first_owner, 0, owners - 1) * h3, h3)], got_z.at[s, off],
            z_s.at[s, off], z_r.at[s, off], device,
        )

    def owned(z):
        return jnp.logical_and(z >= first_owner, z < first_owner + owners)

    def to_owner(off, act):
        pl.when(owned(z_peer(off)[0]))(act)

    for s in range(SLICES):
        value = sum1[s, at(me_mode * h2, h2), :]
        for off, copy in enumerate(stage_m[s]):
            copy.wait_recv()
            value = value + got_m[s, off]
        sends += stage_m[s]
        sum2[s] = value
        each_z(lambda off: to_owner(off, lambda: z_copy(s, off).start()))

    def my_start(s):
        return s * h0 + me_core * h1 + me_mode * h2

    def az_copy(s, off, z):
        _, device = z_peer(off)
        block = tot.at[at(my_start(s) + jnp.clip(z - first_owner, 0, owners - 1) * h3, h3)]
        return remote(block, block, az_s.at[s, off], az_r.at[s, off], device)

    for s in range(SLICES):
        @pl.when(is_owner)
        def _():
            each_z(lambda off: z_copy(s, off).wait_recv())
            spot = at(jnp.clip(me_z - first_owner, 0, owners - 1) * h3, h3)
            value = lax.fori_loop(1, depth, lambda off, v: v + got_z[s, off], sum2[s, spot, :])
            tot[at(my_start(s) + jnp.clip(me_z - first_owner, 0, owners - 1) * h3, h3), :] = value / total_cols
            each_z(lambda off: az_copy(s, off, me_z).start())

    for off, copy in enumerate(stage_d, 1):
        copy.wait_recv()
        source = lax.rem(me_mode - off + modes, modes)
        forward(dtot, at(source * rows_dev + me_core * half, half), df_s.at[off], df_r.at[off])
    sends += stage_d

    stage_a = []
    for s in range(SLICES):
        def arrive(off):
            source = lax.rem(me_z - off + depth, depth)
            pl.when(owned(source))(lambda: az_copy(s, off, source).wait_recv())
        each_z(arrive)
        block = at(my_start(s), h2)
        batch = []
        for off in range(1, modes):
            other, device = mode_peer(off)
            copy = remote(tot.at[block], tot.at[block], am_s.at[s, off], am_r.at[s, off], device)
            copy.start()
            batch.append(copy)
        forward(tot, block, ac_s.at[s, 0], ac_r.at[s, 0])
        stage_a.append(batch)
    for s in range(SLICES):
        for off, copy in enumerate(stage_a[s], 1):
            copy.wait_recv()
            source = lax.rem(me_mode - off + modes, modes)
            forward(tot, at(s * h0 + me_core * h1 + source * h2, h2), ac_s.at[s, off], ac_r.at[s, off])
        sends += stage_a[s]
    for copy in relays:
        copy.wait_recv()

    for i in range(rounds):
        spot = (pl.ds(i * LANES, LANES), pl.ds(i * LANES, LANES))
        piece = dtot[pl.ds(i * LANES, LANES), :]
        gram_ref[spot] = piece
        work[spot] = piece
    for where, (i, j) in enumerate(pairs):
        piece = tot[pl.ds(where * LANES, LANES), :]
        spot = (pl.ds(i * LANES, LANES), pl.ds(j * LANES, LANES))
        gram_ref[spot] = piece
        work[spot] = piece
        gram_ref[spot[::-1]] = piece.T

    r = start_ref.shape[1]

    def refill(basis_t):
        image_t = dotf(basis_t, gram_ref[...], ((1,), (0,)))
        aug[:, pl.ds(0, r)] = dotf(image_t, image_t, ((1,), (1,)))
        aug[:, pl.ds(r, m)] = image_t

    def schur(base):
        tail = m - base - LANES
        u = work[pl.ds(base, LANES), pl.ds(base + LANES, tail)]
        work[pl.ds(base + LANES, tail), pl.ds(base + LANES, tail)] -= dotf(u, u, ((0,), (0,)))

    early = max(rounds - LATE, 0)
    refill(begin[...].T)
    for t in range(max(early, ITERS)):
        base = t * LANES

        def step(block, carry):
            if t < early:
                eliminate(work, base, base, m - base, block)
            if t < ITERS:
                eliminate(aug, 0, 0, r + m, block)
            return carry

        lax.fori_loop(0, LANES // STEP, step, 0)
        if t < early:
            schur(base)
        if t < ITERS - 1:
            refill(aug[:, pl.ds(r, m)])
    basis_t = aug[:, pl.ds(r, m)]
    bh, bl = split(basis_t)
    out_rows = core_ref.shape[0]
    for c, (start, size) in enumerate(cuts(width, SCATTER)):
        cols = pl.ds(start, size)
        xh = hi_ref[:, cols]
        part[:, cols] = nn(bh, xh) + (nn(bh, lo_ref[:, cols]) + nn(bl, xh))
        mine = pl.ds(pl.multiple_of(me_mode * width + start, LANES), size)
        for off in range(1, modes):
            other, device = mode_peer(off)
            copy = remote(
                part.at[at(other * out_rows, out_rows), cols], core_ref.at[:, mine], out_s.at[c, off], out_r.at[c, off], device
            )
            copy.start()
            sends.append(copy)
            arrivals.append([copy])
        core_ref[:, mine] = part[at(me_mode * out_rows, out_rows), cols]
    factor_ref[...] = basis_t.T

    for t in range(early, rounds):
        base = t * LANES

        def late(block, carry):
            eliminate(work, base, base, m - base, block)
            return carry

        lax.fori_loop(0, LANES // STEP, late, 0)
        if t < rounds - 1:
            schur(base)
    row = lax.broadcasted_iota(jnp.int32, (LANES, LANES), 0)
    col = lax.broadcasted_iota(jnp.int32, (LANES, LANES), 1)
    for i in range(rounds):
        for j in range(rounds):
            spot = (pl.ds(j * LANES, LANES), pl.ds(i * LANES, LANES))
            if j < i:
                tri_ref[spot] = jnp.zeros((LANES, LANES), F32)
                continue
            piece = work[spot[::-1]]
            tri_ref[spot] = (jnp.where(row <= col, piece, 0.0) if i == j else piece).T

    for copy in sends:
        copy.wait_send()
    for s in range(SLICES):
        each_z(lambda off: to_owner(off, lambda: z_copy(s, off).wait_send()))

        @pl.when(is_owner)
        def _():
            each_z(lambda off: az_copy(s, off, me_z).wait_send())
    for batch in arrivals[len(pieces):]:
        for copy in batch:
            copy.wait_recv()


def program(unfolded, start_block, modes, rest):
    rows_dev, cols_dev = unfolded.shape
    m, r = start_block.shape
    width = cols_dev // modes
    cores = 2 if rest % 2 == 0 else 1
    depth = rest // cores
    owners = owners_of(depth)[1]
    unit = SLICES * cores * modes * owners * SUB
    padded = pl.cdiv(len(off_pairs(m // LANES)) * LANES, unit) * unit
    h1 = padded // SLICES // cores
    h2 = h1 // modes
    h3 = h2 // owners
    half = rows_dev // cores
    vmem = pl.BlockSpec(memory_space=pltpu.VMEM)
    dma = pltpu.SemaphoreType.DMA
    few = max(cores - 1, 1)
    two = lambda *shape: [dma(shape), dma(shape)]
    return pl.pallas_call(
        functools.partial(kernel, (modes, cores, depth), cols_dev * rest),
        out_shape=(
            jax.ShapeDtypeStruct((m, m), F32),
            jax.ShapeDtypeStruct((m, r), F32),
            jax.ShapeDtypeStruct((r // modes, cols_dev), F32),
        ),
        in_specs=[pl.BlockSpec(memory_space=pltpu.HBM)] * 2,
        out_specs=(vmem, vmem, vmem),
        scratch_shapes=[
            pltpu.VMEM((m, width), F32),
            pltpu.VMEM((m, width), BF16),
            pltpu.VMEM((m, width), BF16),
            pltpu.VMEM((rows_dev, cols_dev), F32),
            pltpu.VMEM((r, width), F32),
            pltpu.VMEM((padded, LANES), F32),
            pltpu.VMEM((padded, LANES), F32),
            pltpu.VMEM((rows_dev, rows_dev), F32),
            pltpu.VMEM((m, LANES), F32),
            pltpu.VMEM((SLICES, few, h1, LANES), F32),
            pltpu.VMEM((SLICES, modes, h2, LANES), F32),
            pltpu.VMEM((SLICES, depth, h3, LANES), F32),
            pltpu.VMEM((SLICES, h1, LANES), F32),
            pltpu.VMEM((SLICES, h2, LANES), F32),
            pltpu.VMEM((few, half, LANES), F32),
            pltpu.VMEM((depth, half, LANES), F32),
            pltpu.VMEM((m, m), F32),
            pltpu.VMEM((m, m), F32),
            pltpu.VMEM((r, r + m), F32),
            pltpu.VMEM((m, r), F32),
            *two(len(GATHER), modes), dma((len(GATHER),)), dma((modes + 1,)),
            *two(SLICES, cores), *two(SLICES, modes), *two(SLICES, depth), *two(SLICES, depth),
            *two(SLICES, modes), *two(SLICES, modes, cores),
            *two(cores), *two(depth), *two(modes), *two(modes, cores),
            *two(len(SCATTER), modes),
        ],
        compiler_params=pltpu.CompilerParams(
            collective_id=0, has_side_effects=True, vmem_limit_bytes=48 * 1024 * 1024
        ),
        name="truncate",
    )(unfolded, start_block)


def per_device(unfolded, start_block):
    return program(unfolded, start_block, lax.axis_size("mode"), lax.axis_size("rest"))


def solution(mesh):
    return jax.shard_map(
        per_device,
        mesh=mesh,
        in_specs=(P("mode", "rest"), P()),
        out_specs=(P(), P(), P("mode", "rest")),
        check_vma=False,
    )
```

```python
import functools

import jax
import jax.numpy as jnp
from jax import lax
from jax.experimental import pallas as pl
from jax.experimental.pallas import tpu as pltpu
from jax.sharding import PartitionSpec as P

ITERS = 3
SUB = 8
MACRO = 32
MICRO = 16
SLICES = 2
LANES = 128
F32 = jnp.float32
BF16 = jnp.bfloat16
MESH = pl.DeviceIdType.MESH


def parts3(x):
    hi = x.astype(BF16).astype(F32)
    rest = x - hi
    mid = rest.astype(BF16).astype(F32)
    return hi, mid, rest - mid


def nt(x, y):
    return lax.dot_general(x, y, (((1,), (1,)), ((), ())), preferred_element_type=F32)


def nn(x, y):
    return lax.dot_general(x, y, (((1,), (0,)), ((), ())), preferred_element_type=F32)


def dotf(x, y, dims):
    return lax.dot_general(
        x, y, (dims, ((), ())), precision=lax.Precision.HIGHEST, preferred_element_type=F32
    )


def spread(x, row):
    return jnp.broadcast_to(x[row : row + 1, :], x.shape)


def column(x, lane):
    return jnp.broadcast_to(x[:, lane : lane + 1], x.shape)


def invert_block(ref, base, r0):
    tiles = MACRO // SUB
    rows = [ref[pl.ds(base + r0 + SUB * h, SUB), :] for h in range(tiles)]
    lane = lax.broadcasted_iota(jnp.int32, (SUB, LANES), 1)
    sub = lax.broadcasted_iota(jnp.int32, (SUB, LANES), 0)
    pivots = [None] * tiles

    def retire(k, f):
        t, s = divmod(k, SUB)
        here = lane == r0 + k
        row = jnp.where(here, 1.0, spread(rows[t], s))
        for h in range(t, tiles):
            if h == t:
                old = jnp.where(here & (sub >= s), jnp.where(sub == s, 1.0, 0.0), rows[h])
            else:
                old = jnp.where(here, 0.0, rows[h])
            rows[h] = old - f[h] * row

    for first in range(0, MACRO, MICRO):
        stop = first + MICRO
        cols = {(j, h): column(rows[h], r0 + j) for j in range(first, stop) for h in range(j // SUB, tiles)}
        unit = spread(cols[first, first // SUB], first % SUB)
        scale = 1.0 / unit
        cols = {spot: x * scale for spot, x in cols.items()}
        for k in range(first, stop, 2):
            t, s = divmod(k, SUB)
            p = spread(cols[k, t], s)
            a = spread(cols[k, t], s + 1)
            b = spread(cols[k + 1, t], s + 1)
            det = p * b - a * a
            inv_p = 1.0 / p
            inv_q = p * (1.0 / det)
            found = jnp.where(sub == s, p, det * inv_p) * unit
            pivots[t] = found if s == 0 else jnp.where(sub >= s, found, pivots[t])
            f = {h: cols[k, h] * inv_p for h in range(t, tiles)}
            f[t] = jnp.where(sub > s, f[t], 0.0)
            second = {h: cols[k + 1, h] - f[h] * a for h in range(t, tiles)}
            g = {h: second[h] * inv_q for h in range(t, tiles)}
            g[t] = jnp.where(sub > s + 1, g[t], 0.0)
            for j in range(k + 2, stop):
                one = spread(cols[k, j // SUB], j % SUB)
                two = spread(second[j // SUB], j % SUB)
                for h in range(j // SUB, tiles):
                    cols[j, h] = (cols[j, h] - f[h] * one) - g[h] * two
            retire(k, f)
            retire(k + 1, g)
    for h in range(tiles):
        s = lax.rsqrt(pivots[h])
        s = s * (1.5 - 0.5 * pivots[h] * s * s)
        rows[h] = rows[h] * s
        ref[pl.ds(base + r0 + SUB * h, SUB), :] = rows[h]
    size = LANES - r0 - MACRO
    if size == 0:
        return
    lane = lax.broadcasted_iota(jnp.int32, (MACRO, LANES), 1)
    row = lax.broadcasted_iota(jnp.int32, (MACRO, LANES), 0)
    keep = lane >= r0 + MACRO
    lower = keep | (lane <= row + r0)
    pieces = parts3(jnp.concatenate(rows, axis=0))
    lh, lm, ll = (jnp.where(keep, x, 0.0) for x in pieces)
    rh, rm, rl = (jnp.where(lower, x, 0.0) for x in pieces)
    left = jnp.concatenate([lh, lh, lm, lm, lh, ll], axis=0).astype(BF16)
    right = jnp.concatenate([rh, rm, rh, rm, rl, rh], axis=0).astype(BF16)
    upd = lax.dot_general(left, right, (((0,), (0,)), ((), ())), preferred_element_type=F32)
    lane = lax.broadcasted_iota(jnp.int32, (size, LANES), 1)
    inside = (lane >= r0) & (lane < r0 + MACRO)
    spot = pl.ds(base + r0 + MACRO, size)
    ref[spot, :] = jnp.where(inside, 0.0, ref[spot, :]) - upd[r0 + MACRO :, :]


def invert(ref, base):
    for r0 in range(0, LANES, MACRO):
        invert_block(ref, base, r0)


def stack(pieces, axis=0):
    return jnp.concatenate(pieces, axis=axis).astype(BF16)


def lower_part(x):
    row = lax.broadcasted_iota(jnp.int32, x.shape, 0)
    col = lax.broadcasted_iota(jnp.int32, x.shape, 1)
    return jnp.where(row >= col, x, 0.0)


def cuts(width, weights):
    unit = width // sum(weights)
    starts = [unit * sum(weights[:k]) for k in range(len(weights))]
    return [(start, unit * weight) for start, weight in zip(starts, weights)]


def split(x):
    hi = x.astype(BF16)
    return hi, (x - hi.astype(F32)).astype(BF16)


def off_pairs(count):
    return [(i, j) for i in range(count) for j in range(i + 1, count)]


def owners_of(depth):
    return (depth // 4, depth // 2) if depth % 4 == 0 else (0, depth)


GATHER = (3, 2, 2, 1)
SCATTER = (1, 1, 2, 2, 2)


def kernel(shape, total_cols, x_ref, start_ref, tri_ref, factor_ref, core_ref,
           full, hi_ref, lo_ref, own, part, acc, tot, dacc, dtot, got_c, got_m, got_z, sum1, sum2, dgot_c, dgot_z,
           work, gram_h, gram_m, gram_l, small, panel, basis, begin,
           row_s, row_r, row_l, own_l, c_s, c_r, m_s, m_r, z_s, z_r, az_s, az_r, am_s, am_r, ac_s, ac_r,
           dc_s, dc_r, dz_s, dz_r, dm_s, dm_r, df_s, df_r, out_s, out_r):
    modes, cores, depth = shape
    me_mode = lax.axis_index("mode")
    me_rest = lax.axis_index("rest")
    me_core = lax.rem(me_rest, cores)
    me_z = me_rest // cores
    first_owner, owners = owners_of(depth)
    is_owner = jnp.logical_and(me_z >= first_owner, me_z < first_owner + owners)
    m, width = full.shape
    rows_dev, cols_dev = x_ref.shape
    rounds = m // LANES

    def mode_peer(off):
        other = lax.rem(me_mode + off, modes)
        return other, (other, me_rest)

    def core_peer(off):
        other = lax.rem(me_core + off, cores)
        return other, (me_mode, me_z * cores + other)

    def z_peer(off):
        other = lax.rem(me_z + off, depth)
        return other, (me_mode, other * cores + me_core)

    def remote(source, target, send, recv, device):
        return pltpu.make_async_remote_copy(
            src_ref=source, dst_ref=target, send_sem=send, recv_sem=recv, device_id=device, device_id_type=MESH
        )

    def at(start, size):
        return pl.ds(pl.multiple_of(start, SUB), size)

    def each_z(body):
        def step(off, carry):
            body(off)
            return carry
        lax.fori_loop(1, depth, step, 0)

    barrier = pltpu.get_barrier_semaphore()
    for peer, size in ((core_peer, cores), (mode_peer, modes)):
        for off in range(1, size):
            pl.semaphore_signal(barrier, inc=1, device_id=peer(off)[1], device_id_type=MESH)
    each_z(lambda off: pl.semaphore_signal(barrier, inc=1, device_id=z_peer(off)[1], device_id_type=MESH))
    pl.semaphore_wait(barrier, modes + cores + depth - 3)

    pieces = cuts(width, GATHER)
    mine_rows = pl.ds(pl.multiple_of(me_mode * rows_dev, rows_dev), rows_dev)
    arrivals = []
    for c, (start, size) in enumerate(pieces):
        spot = (mine_rows, pl.ds(start, size))
        batch = []
        for off in range(1, modes):
            other, device = mode_peer(off)
            batch.append(remote(
                x_ref.at[:, pl.ds(pl.multiple_of(other * width + start, LANES), size)], full.at[spot],
                row_s.at[c, off], row_r.at[c, off], device,
            ))
        batch.append(pltpu.make_async_copy(
            x_ref.at[:, pl.ds(pl.multiple_of(me_mode * width + start, LANES), size)], full.at[spot], row_l.at[c]
        ))
        for copy in batch:
            copy.start()
        arrivals.append(batch)
    loads = []
    for q in range(modes):
        cols = pl.ds(q * width, width)
        load = pltpu.make_async_copy(x_ref.at[:, cols], own.at[:, cols], own_l.at[q])
        load.start()
        loads.append(load)

    fetch = pltpu.make_async_copy(start_ref, begin, own_l.at[modes])
    fetch.start()
    dacc[...] = jnp.zeros_like(dacc)
    acc[...] = jnp.zeros_like(acc)
    for q in range(modes):
        loads[q].wait()
        h, l = split(own[:, pl.ds(q * width, width)])
        cross = nt(h, l)
        dacc[...] += nt(h, h) + (cross + cross.T)
    half = rows_dev // cores
    pending = []
    for off in range(1, cores):
        other, device = core_peer(off)
        copy = remote(dacc.at[at(other * half, half)], dgot_c.at[off - 1], dc_s.at[off], dc_r.at[off], device)
        copy.start()
        pending.append(copy)

    pairs = off_pairs(rounds)

    def absorb(c):
        for copy in arrivals[c]:
            copy.wait()
        start, size = pieces[c]
        cols = pl.ds(start, size)
        hi, lo = split(full[:, cols])
        hi_ref[:, cols] = hi
        lo_ref[:, cols] = lo
        for i in range(rounds - 1):
            top = slice(i * LANES, (i + 1) * LANES)
            rest = slice((i + 1) * LANES, m)
            strip = nt(hi[top], hi[rest]) + (nt(hi[top], lo[rest]) + nt(lo[top], hi[rest]))
            for j in range(i + 1, rounds):
                spot = pl.ds(pairs.index((i, j)) * LANES, LANES)
                acc[spot, :] += strip[:, (j - i - 1) * LANES : (j - i) * LANES]

    absorb(0)
    fetch.wait()
    for copy in pending:
        copy.wait()
    value = dacc[at(me_core * half, half), :]
    for off in range(1, cores):
        value = value + dgot_c[off - 1]
    dgot_z[me_z] = value

    def dz_copy(off):
        _, device = z_peer(off)
        return remote(dgot_z.at[me_z], dgot_z.at[me_z], dz_s.at[off], dz_r.at[off], device)

    each_z(lambda off: dz_copy(off).start())
    absorb(1)
    each_z(lambda off: dz_copy(off).wait())
    value = lax.fori_loop(1, depth, lambda z, v: v + dgot_z[z], dgot_z[0])
    dmine = at(me_mode * rows_dev + me_core * half, half)
    dtot[dmine, :] = value / total_cols
    for c in range(2, len(pieces)):
        absorb(c)

    padded = acc.shape[0]
    h0 = padded // SLICES
    h1 = h0 // cores
    h2 = h1 // modes
    h3 = h2 // owners
    sends = []

    stage_c = []
    for s in range(SLICES):
        batch = []
        for off in range(1, cores):
            other, device = core_peer(off)
            copy = remote(acc.at[at(s * h0 + other * h1, h1)], got_c.at[s, off - 1], c_s.at[s, off], c_r.at[s, off], device)
            copy.start()
            batch.append(copy)
        stage_c.append(batch)
    stage_m = []
    for s in range(SLICES):
        value = acc[at(s * h0 + me_core * h1, h1), :]
        for off, copy in enumerate(stage_c[s]):
            copy.wait_recv()
            value = value + got_c[s, off]
        sends += stage_c[s]
        sum1[s] = value
        batch = []
        for off in range(1, modes):
            other, device = mode_peer(off)
            copy = remote(sum1.at[s, at(other * h2, h2)], got_m.at[s, off - 1], m_s.at[s, off], m_r.at[s, off], device)
            copy.start()
            batch.append(copy)
        stage_m.append(batch)
    stage_d = []
    for off in range(1, modes):
        other, device = mode_peer(off)
        copy = remote(dtot.at[dmine], dtot.at[dmine], dm_s.at[off], dm_r.at[off], device)
        copy.start()
        stage_d.append(copy)

    def forward(ref, spot, send, recv):
        for off in range(1, cores):
            _, device = core_peer(off)
            copy = remote(ref.at[spot], ref.at[spot], send.at[off], recv.at[off], device)
            copy.start()
            sends.append(copy)
            relays.append(copy)

    relays = []

    def keep_gram(spot, piece):
        for ref, value in zip((gram_h, gram_m, gram_l), parts3(piece)):
            ref[spot] = value.astype(BF16)

    forward(dtot, dmine, df_s.at[0], df_r.at[0])

    def z_copy(s, off):
        other, device = z_peer(off)
        return remote(
            sum2.at[s, at(jnp.clip(other - first_owner, 0, owners - 1) * h3, h3)], got_z.at[s, off],
            z_s.at[s, off], z_r.at[s, off], device,
        )

    def owned(z):
        return jnp.logical_and(z >= first_owner, z < first_owner + owners)

    def to_owner(off, act):
        pl.when(owned(z_peer(off)[0]))(act)

    for s in range(SLICES):
        value = sum1[s, at(me_mode * h2, h2), :]
        for off, copy in enumerate(stage_m[s]):
            copy.wait_recv()
            value = value + got_m[s, off]
        sends += stage_m[s]
        sum2[s] = value
        each_z(lambda off: to_owner(off, lambda: z_copy(s, off).start()))

    def my_start(s):
        return s * h0 + me_core * h1 + me_mode * h2

    def az_copy(s, off, z):
        _, device = z_peer(off)
        block = tot.at[at(my_start(s) + jnp.clip(z - first_owner, 0, owners - 1) * h3, h3)]
        return remote(block, block, az_s.at[s, off], az_r.at[s, off], device)

    for s in range(SLICES):
        @pl.when(is_owner)
        def _():
            each_z(lambda off: z_copy(s, off).wait_recv())
            spot = at(jnp.clip(me_z - first_owner, 0, owners - 1) * h3, h3)
            value = lax.fori_loop(1, depth, lambda off, v: v + got_z[s, off], sum2[s, spot, :])
            tot[at(my_start(s) + jnp.clip(me_z - first_owner, 0, owners - 1) * h3, h3), :] = value / total_cols
            each_z(lambda off: az_copy(s, off, me_z).start())

    for off, copy in enumerate(stage_d, 1):
        copy.wait_recv()
        source = lax.rem(me_mode - off + modes, modes)
        forward(dtot, at(source * rows_dev + me_core * half, half), df_s.at[off], df_r.at[off])
    sends += stage_d
    for copy in relays:
        copy.wait_recv()
    relays.clear()
    for i in range(rounds):
        spot = (pl.ds(i * LANES, LANES), pl.ds(i * LANES, LANES))
        piece = dtot[pl.ds(i * LANES, LANES), :]
        keep_gram(spot, piece)
        work[spot] = piece
    panel[pl.ds(0, LANES), :] = dtot[pl.ds(0, LANES), :]
    invert(panel, 0)

    stage_a = []
    for s in range(SLICES):
        def arrive(off):
            source = lax.rem(me_z - off + depth, depth)
            pl.when(owned(source))(lambda: az_copy(s, off, source).wait_recv())
        each_z(arrive)
        block = at(my_start(s), h2)
        batch = []
        for off in range(1, modes):
            other, device = mode_peer(off)
            copy = remote(tot.at[block], tot.at[block], am_s.at[s, off], am_r.at[s, off], device)
            copy.start()
            batch.append(copy)
        forward(tot, block, ac_s.at[s, 0], ac_r.at[s, 0])
        stage_a.append(batch)
    for s in range(SLICES):
        for off, copy in enumerate(stage_a[s], 1):
            copy.wait_recv()
            source = lax.rem(me_mode - off + modes, modes)
            forward(tot, at(s * h0 + me_core * h1 + source * h2, h2), ac_s.at[s, off], ac_r.at[s, off])
        sends += stage_a[s]
    for copy in relays:
        copy.wait_recv()

    for where, (i, j) in enumerate(pairs):
        piece = tot[pl.ds(where * LANES, LANES), :]
        spot = (pl.ds(i * LANES, LANES), pl.ds(j * LANES, LANES))
        work[spot] = piece
        keep_gram(spot, piece)
        keep_gram(spot[::-1], piece.T)

    basis[...] = begin[...].T
    r = basis.shape[0]

    def iterate(t, carry):
        old = stack(parts3(basis[...]))
        one = nn(old, gram_h[...])
        two = nn(old[: 2 * r], gram_m[...])
        image = one[:r] + ((one[r : 2 * r] + two[:r]) + (one[2 * r :] + (two[r:] + nn(old[:r], gram_l[...]))))
        ih, im, il = parts3(image)
        new = stack([ih, im, il])
        q = nt(new, new[: 2 * r])
        low = q[2 * r :, :r]
        small[...] = q[:r, :r] + ((q[:r, r:] + q[r : 2 * r, :r]) + (q[r : 2 * r, r:] + (low + low.T)))
        invert(small, 0)
        wh, wm, wl = parts3(lower_part(small[...]))
        high = nn(stack([stack([wh, wh], 1), stack([wm, wm], 1)]), new[: 2 * r])
        rest = nn(stack([wl, wh], 1), stack([ih, il]))
        basis[...] = high[:r] + (high[r:] + rest)
        return carry

    lax.fori_loop(0, ITERS, iterate, 0)
    basis_t = basis[...]
    bh, bl = split(basis_t)
    out_rows = core_ref.shape[0]
    for c, (start, size) in enumerate(cuts(width, SCATTER)):
        cols = pl.ds(start, size)
        xh = hi_ref[:, cols]
        part[:, cols] = nn(bh, xh) + (nn(bh, lo_ref[:, cols]) + nn(bl, xh))
        mine = pl.ds(pl.multiple_of(me_mode * width + start, LANES), size)
        for off in range(1, modes):
            other, device = mode_peer(off)
            copy = remote(
                part.at[at(other * out_rows, out_rows), cols], core_ref.at[:, mine], out_s.at[c, off], out_r.at[c, off], device
            )
            copy.start()
            sends.append(copy)
            arrivals.append([copy])
        core_ref[:, mine] = part[at(me_mode * out_rows, out_rows), cols]
    factor_ref[...] = basis_t.T

    for t in range(rounds):
        base = t * LANES
        here = pl.ds(base, LANES)
        if t > 0:
            panel[here, :] = work[here, here]
            invert(panel, base)
        if t < rounds - 1:
            tail = pl.ds(base + LANES, m - base - LANES)
            u = dotf(lower_part(panel[here, :]), work[here, tail], ((1,), (0,)))
            work[here, tail] = u
            work[tail, tail] -= dotf(u, u, ((0,), (0,)))
    row = lax.broadcasted_iota(jnp.int32, (LANES, LANES), 0)
    col = lax.broadcasted_iota(jnp.int32, (LANES, LANES), 1)
    for i in range(rounds):
        for j in range(rounds):
            spot = (pl.ds(j * LANES, LANES), pl.ds(i * LANES, LANES))
            if j < i:
                tri_ref[spot] = jnp.zeros((LANES, LANES), F32)
            elif j > i:
                tri_ref[spot] = work[spot[::-1]].T
            else:
                piece = panel[pl.ds(i * LANES, LANES), :]
                tri_ref[spot] = jnp.where(row < col, piece, jnp.where(row == col, 1.0 / piece, 0.0)).T

    for copy in sends:
        copy.wait_send()
    for s in range(SLICES):
        each_z(lambda off: to_owner(off, lambda: z_copy(s, off).wait_send()))

        @pl.when(is_owner)
        def _():
            each_z(lambda off: az_copy(s, off, me_z).wait_send())
    for batch in arrivals[len(pieces):]:
        for copy in batch:
            copy.wait_recv()


def program(unfolded, start_block, modes, rest):
    rows_dev, cols_dev = unfolded.shape
    m, r = start_block.shape
    width = cols_dev // modes
    cores = 2 if rest % 2 == 0 else 1
    depth = rest // cores
    owners = owners_of(depth)[1]
    unit = SLICES * cores * modes * owners * SUB
    padded = pl.cdiv(len(off_pairs(m // LANES)) * LANES, unit) * unit
    h1 = padded // SLICES // cores
    h2 = h1 // modes
    h3 = h2 // owners
    half = rows_dev // cores
    vmem = pl.BlockSpec(memory_space=pltpu.VMEM)
    dma = pltpu.SemaphoreType.DMA
    few = max(cores - 1, 1)
    two = lambda *shape: [dma(shape), dma(shape)]
    return pl.pallas_call(
        functools.partial(kernel, (modes, cores, depth), cols_dev * rest),
        out_shape=(
            jax.ShapeDtypeStruct((m, m), F32),
            jax.ShapeDtypeStruct((m, r), F32),
            jax.ShapeDtypeStruct((r // modes, cols_dev), F32),
        ),
        in_specs=[pl.BlockSpec(memory_space=pltpu.HBM)] * 2,
        out_specs=(vmem, vmem, vmem),
        scratch_shapes=[
            pltpu.VMEM((m, width), F32),
            pltpu.VMEM((m, width), BF16),
            pltpu.VMEM((m, width), BF16),
            pltpu.VMEM((rows_dev, cols_dev), F32),
            pltpu.VMEM((r, width), F32),
            pltpu.VMEM((padded, LANES), F32),
            pltpu.VMEM((padded, LANES), F32),
            pltpu.VMEM((rows_dev, rows_dev), F32),
            pltpu.VMEM((m, LANES), F32),
            pltpu.VMEM((SLICES, few, h1, LANES), F32),
            pltpu.VMEM((SLICES, modes, h2, LANES), F32),
            pltpu.VMEM((SLICES, depth, h3, LANES), F32),
            pltpu.VMEM((SLICES, h1, LANES), F32),
            pltpu.VMEM((SLICES, h2, LANES), F32),
            pltpu.VMEM((few, half, LANES), F32),
            pltpu.VMEM((depth, half, LANES), F32),
            pltpu.VMEM((m, m), F32),
            *[pltpu.VMEM((m, m), BF16)] * 3,
            pltpu.VMEM((r, r), F32),
            pltpu.VMEM((m, LANES), F32),
            pltpu.VMEM((r, m), F32),
            pltpu.VMEM((m, r), F32),
            *two(len(GATHER), modes), dma((len(GATHER),)), dma((modes + 1,)),
            *two(SLICES, cores), *two(SLICES, modes), *two(SLICES, depth), *two(SLICES, depth),
            *two(SLICES, modes), *two(SLICES, modes, cores),
            *two(cores), *two(depth), *two(modes), *two(modes, cores),
            *two(len(SCATTER), modes),
        ],
        compiler_params=pltpu.CompilerParams(
            collective_id=0, has_side_effects=True, vmem_limit_bytes=48 * 1024 * 1024
        ),
        name="truncate",
    )(unfolded, start_block)


def emit_kernel(*refs):
    count = len(refs) // 2
    sem = refs[-1]
    copies = [pltpu.make_async_copy(refs[k], refs[count + k], sem.at[k]) for k in range(count)]
    for copy in copies:
        copy.start()
    for copy in copies:
        copy.wait()


def emit(*arrays):
    count = len(arrays)
    return pl.pallas_call(
        emit_kernel,
        out_shape=tuple(jax.ShapeDtypeStruct(x.shape, x.dtype) for x in arrays),
        in_specs=[pl.BlockSpec(memory_space=pl.ANY)] * count,
        out_specs=(pl.BlockSpec(memory_space=pltpu.HBM),) * count,
        scratch_shapes=[pltpu.SemaphoreType.DMA((count,))],
        compiler_params=pltpu.CompilerParams(vmem_limit_bytes=1024 * 1024),
        name="emit",
    )(*arrays)


def per_device(unfolded, start_block):
    return emit(*program(unfolded, start_block, lax.axis_size("mode"), lax.axis_size("rest")))


def solution(mesh):
    return jax.shard_map(
        per_device,
        mesh=mesh,
        in_specs=(P("mode", "rest"), P()),
        out_specs=(P(), P(), P("mode", "rest")),
        check_vma=False,
    )
```

```python
import functools

import jax
import jax.numpy as jnp
from jax import lax
from jax.experimental import pallas as pl
from jax.experimental.pallas import tpu as pltpu
from jax.sharding import PartitionSpec as P

ITERS = 3
SUB = 8
MACRO = 32
MICRO = 16
SLICES = 2
LANES = 128
F32 = jnp.float32
BF16 = jnp.bfloat16
MESH = pl.DeviceIdType.MESH


def parts3(x):
    hi = x.astype(BF16).astype(F32)
    rest = x - hi
    mid = rest.astype(BF16).astype(F32)
    return hi, mid, rest - mid


def nt(x, y):
    return lax.dot_general(x, y, (((1,), (1,)), ((), ())), preferred_element_type=F32)


def nn(x, y):
    return lax.dot_general(x, y, (((1,), (0,)), ((), ())), preferred_element_type=F32)


def dotf(x, y, dims):
    return lax.dot_general(
        x, y, (dims, ((), ())), precision=lax.Precision.HIGHEST, preferred_element_type=F32
    )


def spread(x, row):
    return jnp.broadcast_to(x[row : row + 1, :], x.shape)


def column(x, lane):
    return jnp.broadcast_to(x[:, lane : lane + 1], x.shape)


def invert_block(ref, base, r0):
    tiles = MACRO // SUB
    rows = [ref[pl.ds(base + r0 + SUB * h, SUB), :] for h in range(tiles)]
    lane = lax.broadcasted_iota(jnp.int32, (SUB, LANES), 1)
    sub = lax.broadcasted_iota(jnp.int32, (SUB, LANES), 0)
    pivots = [None] * tiles

    def retire(k, f):
        t, s = divmod(k, SUB)
        here = lane == r0 + k
        row = jnp.where(here, 1.0, spread(rows[t], s))
        for h in range(t, tiles):
            if h == t:
                old = jnp.where(here & (sub >= s), jnp.where(sub == s, 1.0, 0.0), rows[h])
            else:
                old = jnp.where(here, 0.0, rows[h])
            rows[h] = old - f[h] * row

    for first in range(0, MACRO, MICRO):
        stop = first + MICRO
        cols = {(j, h): column(rows[h], r0 + j) for j in range(first, stop) for h in range(j // SUB, tiles)}
        unit = spread(cols[first, first // SUB], first % SUB)
        scale = 1.0 / unit
        cols = {spot: x * scale for spot, x in cols.items()}
        for k in range(first, stop, 2):
            t, s = divmod(k, SUB)
            p = spread(cols[k, t], s)
            a = spread(cols[k, t], s + 1)
            b = spread(cols[k + 1, t], s + 1)
            det = p * b - a * a
            inv_p = 1.0 / p
            inv_q = p * (1.0 / det)
            found = jnp.where(sub == s, p, det * inv_p) * unit
            pivots[t] = found if s == 0 else jnp.where(sub >= s, found, pivots[t])
            f = {h: cols[k, h] * inv_p for h in range(t, tiles)}
            f[t] = jnp.where(sub > s, f[t], 0.0)
            second = {h: cols[k + 1, h] - f[h] * a for h in range(t, tiles)}
            g = {h: second[h] * inv_q for h in range(t, tiles)}
            g[t] = jnp.where(sub > s + 1, g[t], 0.0)
            for j in range(k + 2, stop):
                one = spread(cols[k, j // SUB], j % SUB)
                two = spread(second[j // SUB], j % SUB)
                for h in range(j // SUB, tiles):
                    cols[j, h] = (cols[j, h] - f[h] * one) - g[h] * two
            retire(k, f)
            retire(k + 1, g)
    for h in range(tiles):
        s = lax.rsqrt(pivots[h])
        s = s * (1.5 - 0.5 * pivots[h] * s * s)
        rows[h] = rows[h] * s
        ref[pl.ds(base + r0 + SUB * h, SUB), :] = rows[h]
    size = LANES - r0 - MACRO
    if size == 0:
        return
    lane = lax.broadcasted_iota(jnp.int32, (MACRO, LANES), 1)
    row = lax.broadcasted_iota(jnp.int32, (MACRO, LANES), 0)
    keep = lane >= r0 + MACRO
    lower = keep | (lane <= row + r0)
    pieces = parts3(jnp.concatenate(rows, axis=0))
    lh, lm, ll = (jnp.where(keep, x, 0.0) for x in pieces)
    rh, rm, rl = (jnp.where(lower, x, 0.0) for x in pieces)
    left = jnp.concatenate([lh, lh, lm, lm, lh, ll], axis=0).astype(BF16)
    right = jnp.concatenate([rh, rm, rh, rm, rl, rh], axis=0).astype(BF16)
    upd = lax.dot_general(left, right, (((0,), (0,)), ((), ())), preferred_element_type=F32)
    lane = lax.broadcasted_iota(jnp.int32, (size, LANES), 1)
    inside = (lane >= r0) & (lane < r0 + MACRO)
    spot = pl.ds(base + r0 + MACRO, size)
    ref[spot, :] = jnp.where(inside, 0.0, ref[spot, :]) - upd[r0 + MACRO :, :]


def invert(ref, base):
    for r0 in range(0, LANES, MACRO):
        invert_block(ref, base, r0)


def stack(pieces, axis=0):
    return jnp.concatenate(pieces, axis=axis).astype(BF16)


def lower_part(x):
    row = lax.broadcasted_iota(jnp.int32, x.shape, 0)
    col = lax.broadcasted_iota(jnp.int32, x.shape, 1)
    return jnp.where(row >= col, x, 0.0)


def cuts(width, weights):
    unit = width // sum(weights)
    starts = [unit * sum(weights[:k]) for k in range(len(weights))]
    return [(start, unit * weight) for start, weight in zip(starts, weights)]


def split(x):
    hi = x.astype(BF16)
    return hi, (x - hi.astype(F32)).astype(BF16)


def off_pairs(count):
    return [(i, j) for i in range(count) for j in range(i + 1, count)]


def owners_of(depth):
    return (depth // 4, depth // 2) if depth % 4 == 0 else (0, depth)


GATHER = (6, 4, 3, 2, 1)
SCATTER = (1, 1, 2, 2, 2)


def kernel(shape, total_cols, x_ref, start_ref, tri_ref, factor_ref, core_ref,
           full, hi_ref, lo_ref, own, part, acc, tot, dacc, dtot, got_c, got_m, got_z, sum1, sum2, dgot_c, dgot_z,
           work, gram_h, gram_m, gram_l, small, panel, basis, pieces_ref, begin,
           row_s, row_r, row_l, own_l, c_s, c_r, m_s, m_r, z_s, z_r, az_s, az_r, am_s, am_r, ac_s, ac_r,
           dc_s, dc_r, dz_s, dz_r, dm_s, dm_r, df_s, df_r, out_s, out_r):
    modes, cores, depth = shape
    me_mode = lax.axis_index("mode")
    me_rest = lax.axis_index("rest")
    me_core = lax.rem(me_rest, cores)
    me_z = me_rest // cores
    first_owner, owners = owners_of(depth)
    is_owner = jnp.logical_and(me_z >= first_owner, me_z < first_owner + owners)
    m, width = full.shape
    rows_dev, cols_dev = x_ref.shape
    rounds = m // LANES

    def mode_peer(off):
        other = lax.rem(me_mode + off, modes)
        return other, (other, me_rest)

    def core_peer(off):
        other = lax.rem(me_core + off, cores)
        return other, (me_mode, me_z * cores + other)

    def z_peer(off):
        other = lax.rem(me_z + off, depth)
        return other, (me_mode, other * cores + me_core)

    def remote(source, target, send, recv, device):
        return pltpu.make_async_remote_copy(
            src_ref=source, dst_ref=target, send_sem=send, recv_sem=recv, device_id=device, device_id_type=MESH
        )

    def at(start, size):
        return pl.ds(pl.multiple_of(start, SUB), size)

    def each_z(body):
        def step(off, carry):
            body(off)
            return carry
        lax.fori_loop(1, depth, step, 0)

    barrier = pltpu.get_barrier_semaphore()
    for peer, size in ((core_peer, cores), (mode_peer, modes)):
        for off in range(1, size):
            pl.semaphore_signal(barrier, inc=1, device_id=peer(off)[1], device_id_type=MESH)
    each_z(lambda off: pl.semaphore_signal(barrier, inc=1, device_id=z_peer(off)[1], device_id_type=MESH))
    pl.semaphore_wait(barrier, modes + cores + depth - 3)

    pieces = cuts(width, GATHER)
    mine_rows = pl.ds(pl.multiple_of(me_mode * rows_dev, rows_dev), rows_dev)
    arrivals = []
    for c, (start, size) in enumerate(pieces):
        spot = (mine_rows, pl.ds(start, size))
        batch = []
        for off in range(1, modes):
            other, device = mode_peer(off)
            batch.append(remote(
                x_ref.at[:, pl.ds(pl.multiple_of(other * width + start, LANES), size)], full.at[spot],
                row_s.at[c, off], row_r.at[c, off], device,
            ))
        batch.append(pltpu.make_async_copy(
            x_ref.at[:, pl.ds(pl.multiple_of(me_mode * width + start, LANES), size)], full.at[spot], row_l.at[c]
        ))
        for copy in batch:
            copy.start()
        arrivals.append(batch)
    loads = []
    for q in range(modes):
        cols = pl.ds(q * width, width)
        load = pltpu.make_async_copy(x_ref.at[:, cols], own.at[:, cols], own_l.at[q])
        load.start()
        loads.append(load)

    fetch = pltpu.make_async_copy(start_ref, begin, own_l.at[modes])
    fetch.start()
    dacc[...] = jnp.zeros_like(dacc)
    acc[...] = jnp.zeros_like(acc)
    for q in range(modes):
        loads[q].wait()
        h, l = split(own[:, pl.ds(q * width, width)])
        cross = nt(h, l)
        dacc[...] += nt(h, h) + (cross + cross.T)
    half = rows_dev // cores
    pending = []
    for off in range(1, cores):
        other, device = core_peer(off)
        copy = remote(dacc.at[at(other * half, half)], dgot_c.at[off - 1], dc_s.at[off], dc_r.at[off], device)
        copy.start()
        pending.append(copy)

    pairs = off_pairs(rounds)

    padded = acc.shape[0]
    h0 = padded // SLICES
    h1 = h0 // cores
    h2 = h1 // modes
    h3 = h2 // owners
    sends = []
    stage_c = []

    def begin_slice(s):
        batch = []
        for off in range(1, cores):
            other, device = core_peer(off)
            copy = remote(acc.at[at(s * h0 + other * h1, h1)], got_c.at[s, off - 1], c_s.at[s, off], c_r.at[s, off], device)
            copy.start()
            batch.append(copy)
        stage_c.append(batch)

    def absorb(c):
        for copy in arrivals[c]:
            copy.wait()
        start, size = pieces[c]
        cols = pl.ds(start, size)
        hi, lo = split(full[:, cols])
        hi_ref[:, cols] = hi
        lo_ref[:, cols] = lo
        for i in range(rounds - 1):
            top = slice(i * LANES, (i + 1) * LANES)
            rest = slice((i + 1) * LANES, m)
            strip = nt(hi[top], hi[rest]) + (nt(hi[top], lo[rest]) + nt(lo[top], hi[rest]))
            for j in range(i + 1, rounds):
                spot = pl.ds(pairs.index((i, j)) * LANES, LANES)
                acc[spot, :] += strip[:, (j - i - 1) * LANES : (j - i) * LANES]
            if c == len(pieces) - 1:
                done = len([p for p in pairs if p[0] <= i]) * LANES
                while (len(stage_c) + 1) * h0 <= done:
                    begin_slice(len(stage_c))

    absorb(0)
    fetch.wait()
    pieces_ref[...] = stack(parts3(begin[...].T))
    for copy in pending:
        copy.wait()
    value = dacc[at(me_core * half, half), :]
    for off in range(1, cores):
        value = value + dgot_c[off - 1]
    dgot_z[me_z] = value

    def dz_copy(off):
        _, device = z_peer(off)
        return remote(dgot_z.at[me_z], dgot_z.at[me_z], dz_s.at[off], dz_r.at[off], device)

    each_z(lambda off: dz_copy(off).start())
    absorb(1)
    each_z(lambda off: dz_copy(off).wait())
    value = lax.fori_loop(1, depth, lambda z, v: v + dgot_z[z], dgot_z[0])
    dmine = at(me_mode * rows_dev + me_core * half, half)
    dtot[dmine, :] = value / total_cols
    for c in range(2, len(pieces)):
        absorb(c)

    for s in range(len(stage_c), SLICES):
        begin_slice(s)
    stage_m = []
    for s in range(SLICES):
        value = acc[at(s * h0 + me_core * h1, h1), :]
        for off, copy in enumerate(stage_c[s]):
            copy.wait_recv()
            value = value + got_c[s, off]
        sends += stage_c[s]
        sum1[s] = value
        batch = []
        for off in range(1, modes):
            other, device = mode_peer(off)
            copy = remote(sum1.at[s, at(other * h2, h2)], got_m.at[s, off - 1], m_s.at[s, off], m_r.at[s, off], device)
            copy.start()
            batch.append(copy)
        stage_m.append(batch)
    stage_d = []
    for off in range(1, modes):
        other, device = mode_peer(off)
        copy = remote(dtot.at[dmine], dtot.at[dmine], dm_s.at[off], dm_r.at[off], device)
        copy.start()
        stage_d.append(copy)

    def forward(relays, ref, spot, send, recv):
        for off in range(1, cores):
            _, device = core_peer(off)
            copy = remote(ref.at[spot], ref.at[spot], send.at[off], recv.at[off], device)
            copy.start()
            sends.append(copy)
            relays.append(copy)

    relays = []

    def keep_gram(spot, piece):
        for ref, value in zip((gram_h, gram_m, gram_l), parts3(piece)):
            ref[spot] = value.astype(BF16)

    forward(relays, dtot, dmine, df_s.at[0], df_r.at[0])

    def z_copy(s, off):
        other, device = z_peer(off)
        return remote(
            sum2.at[s, at(jnp.clip(other - first_owner, 0, owners - 1) * h3, h3)], got_z.at[s, off],
            z_s.at[s, off], z_r.at[s, off], device,
        )

    def owned(z):
        return jnp.logical_and(z >= first_owner, z < first_owner + owners)

    def to_owner(off, act):
        pl.when(owned(z_peer(off)[0]))(act)

    for s in range(SLICES):
        value = sum1[s, at(me_mode * h2, h2), :]
        for off, copy in enumerate(stage_m[s]):
            copy.wait_recv()
            value = value + got_m[s, off]
        sends += stage_m[s]
        sum2[s] = value
        each_z(lambda off: to_owner(off, lambda: z_copy(s, off).start()))

    def my_start(s):
        return s * h0 + me_core * h1 + me_mode * h2

    def az_copy(s, off, z):
        _, device = z_peer(off)
        block = tot.at[at(my_start(s) + jnp.clip(z - first_owner, 0, owners - 1) * h3, h3)]
        return remote(block, block, az_s.at[s, off], az_r.at[s, off], device)

    for s in range(SLICES):
        @pl.when(is_owner)
        def _():
            each_z(lambda off: z_copy(s, off).wait_recv())
            spot = at(jnp.clip(me_z - first_owner, 0, owners - 1) * h3, h3)
            value = lax.fori_loop(1, depth, lambda off, v: v + got_z[s, off], sum2[s, spot, :])
            tot[at(my_start(s) + jnp.clip(me_z - first_owner, 0, owners - 1) * h3, h3), :] = value / total_cols
            each_z(lambda off: az_copy(s, off, me_z).start())

    for off, copy in enumerate(stage_d, 1):
        copy.wait_recv()
        source = lax.rem(me_mode - off + modes, modes)
        forward(relays, dtot, at(source * rows_dev + me_core * half, half), df_s.at[off], df_r.at[off])
    sends += stage_d
    for copy in relays:
        copy.wait_recv()
    for i in range(rounds):
        spot = (pl.ds(i * LANES, LANES), pl.ds(i * LANES, LANES))
        piece = dtot[pl.ds(i * LANES, LANES), :]
        keep_gram(spot, piece)
        work[spot] = piece
    panel[pl.ds(0, LANES), :] = dtot[pl.ds(0, LANES), :]
    invert(panel, 0)

    stage_a = []
    hops = []
    for s in range(SLICES):
        def arrive(off):
            source = lax.rem(me_z - off + depth, depth)
            pl.when(owned(source))(lambda: az_copy(s, off, source).wait_recv())
        each_z(arrive)
        block = at(my_start(s), h2)
        batch = []
        for off in range(1, modes):
            other, device = mode_peer(off)
            copy = remote(tot.at[block], tot.at[block], am_s.at[s, off], am_r.at[s, off], device)
            copy.start()
            batch.append(copy)
        hops.append([])
        forward(hops[s], tot, block, ac_s.at[s, 0], ac_r.at[s, 0])
        stage_a.append(batch)
    for s in range(SLICES):
        for off, copy in enumerate(stage_a[s], 1):
            copy.wait_recv()
            source = lax.rem(me_mode - off + modes, modes)
            forward(hops[s], tot, at(s * h0 + me_core * h1 + source * h2, h2), ac_s.at[s, off], ac_r.at[s, off])
        sends += stage_a[s]
    for s in range(SLICES):
        for copy in hops[s]:
            copy.wait_recv()
        for where, (i, j) in enumerate(pairs):
            if (where * LANES + LANES - 1) // h0 == s:
                piece = tot[pl.ds(where * LANES, LANES), :]
                spot = (pl.ds(i * LANES, LANES), pl.ds(j * LANES, LANES))
                work[spot] = piece
                keep_gram(spot, piece)
                keep_gram(spot[::-1], piece.T)

    r = basis.shape[0]

    def iterate(t, carry):
        old = pieces_ref[...]
        one = nn(old, gram_h[...])
        two = nn(old[: 2 * r], gram_m[...])
        image = one[:r] + ((one[r : 2 * r] + two[:r]) + (one[2 * r :] + (two[r:] + nn(old[:r], gram_l[...]))))
        ih, im, il = parts3(image)
        new = stack([ih, im, il])
        q = nt(new, new[: 2 * r])
        low = q[2 * r :, :r]
        small[...] = q[:r, :r] + ((q[:r, r:] + q[r : 2 * r, :r]) + (q[r : 2 * r, r:] + (low + low.T)))
        invert(small, 0)
        wh, wm, wl = parts3(lower_part(small[...]))
        high = nn(stack([stack([wh, wh], 1), stack([wm, wm], 1)]), new[: 2 * r])
        rest = nn(stack([wl, wh], 1), stack([ih, il]))
        result = high[:r] + (high[r:] + rest)
        basis[...] = result
        pieces_ref[...] = stack(parts3(result))
        return carry

    lax.fori_loop(0, ITERS, iterate, 0)
    basis_t = basis[...]
    bh, bl = pieces_ref[:r, :], pieces_ref[r : 2 * r, :]
    out_rows = core_ref.shape[0]
    for c, (start, size) in enumerate(cuts(width, SCATTER)):
        cols = pl.ds(start, size)
        xh = hi_ref[:, cols]
        part[:, cols] = nn(bh, xh) + (nn(bh, lo_ref[:, cols]) + nn(bl, xh))
        mine = pl.ds(pl.multiple_of(me_mode * width + start, LANES), size)
        for off in range(1, modes):
            other, device = mode_peer(off)
            copy = remote(
                part.at[at(other * out_rows, out_rows), cols], core_ref.at[:, mine], out_s.at[c, off], out_r.at[c, off], device
            )
            copy.start()
            sends.append(copy)
            arrivals.append([copy])
        core_ref[:, mine] = part[at(me_mode * out_rows, out_rows), cols]
    factor_ref[...] = basis_t.T

    for t in range(rounds):
        base = t * LANES
        here = pl.ds(base, LANES)
        if t > 0:
            panel[here, :] = work[here, here]
            invert(panel, base)
        if t < rounds - 1:
            tail = pl.ds(base + LANES, m - base - LANES)
            u = dotf(lower_part(panel[here, :]), work[here, tail], ((1,), (0,)))
            work[here, tail] = u
            work[tail, tail] -= dotf(u, u, ((0,), (0,)))
    row = lax.broadcasted_iota(jnp.int32, (LANES, LANES), 0)
    col = lax.broadcasted_iota(jnp.int32, (LANES, LANES), 1)
    for i in range(rounds):
        for j in range(rounds):
            spot = (pl.ds(j * LANES, LANES), pl.ds(i * LANES, LANES))
            if j < i:
                tri_ref[spot] = jnp.zeros((LANES, LANES), F32)
            elif j > i:
                tri_ref[spot] = work[spot[::-1]].T
            else:
                piece = panel[pl.ds(i * LANES, LANES), :]
                tri_ref[spot] = jnp.where(row < col, piece, jnp.where(row == col, 1.0 / piece, 0.0)).T

    for copy in sends:
        copy.wait_send()
    for s in range(SLICES):
        each_z(lambda off: to_owner(off, lambda: z_copy(s, off).wait_send()))

        @pl.when(is_owner)
        def _():
            each_z(lambda off: az_copy(s, off, me_z).wait_send())
    for batch in arrivals[len(pieces):]:
        for copy in batch:
            copy.wait_recv()


def program(unfolded, start_block, modes, rest):
    rows_dev, cols_dev = unfolded.shape
    m, r = start_block.shape
    width = cols_dev // modes
    cores = 2 if rest % 2 == 0 else 1
    depth = rest // cores
    owners = owners_of(depth)[1]
    unit = SLICES * cores * modes * owners * SUB
    padded = pl.cdiv(len(off_pairs(m // LANES)) * LANES, unit) * unit
    h1 = padded // SLICES // cores
    h2 = h1 // modes
    h3 = h2 // owners
    half = rows_dev // cores
    vmem = pl.BlockSpec(memory_space=pltpu.VMEM)
    dma = pltpu.SemaphoreType.DMA
    few = max(cores - 1, 1)
    two = lambda *shape: [dma(shape), dma(shape)]
    return pl.pallas_call(
        functools.partial(kernel, (modes, cores, depth), cols_dev * rest),
        out_shape=(
            jax.ShapeDtypeStruct((m, m), F32),
            jax.ShapeDtypeStruct((m, r), F32),
            jax.ShapeDtypeStruct((r // modes, cols_dev), F32),
        ),
        in_specs=[pl.BlockSpec(memory_space=pltpu.HBM)] * 2,
        out_specs=(vmem, vmem, vmem),
        scratch_shapes=[
            pltpu.VMEM((m, width), F32),
            pltpu.VMEM((m, width), BF16),
            pltpu.VMEM((m, width), BF16),
            pltpu.VMEM((rows_dev, cols_dev), F32),
            pltpu.VMEM((r, width), F32),
            pltpu.VMEM((padded, LANES), F32),
            pltpu.VMEM((padded, LANES), F32),
            pltpu.VMEM((rows_dev, rows_dev), F32),
            pltpu.VMEM((m, LANES), F32),
            pltpu.VMEM((SLICES, few, h1, LANES), F32),
            pltpu.VMEM((SLICES, modes, h2, LANES), F32),
            pltpu.VMEM((SLICES, depth, h3, LANES), F32),
            pltpu.VMEM((SLICES, h1, LANES), F32),
            pltpu.VMEM((SLICES, h2, LANES), F32),
            pltpu.VMEM((few, half, LANES), F32),
            pltpu.VMEM((depth, half, LANES), F32),
            pltpu.VMEM((m, m), F32),
            *[pltpu.VMEM((m, m), BF16)] * 3,
            pltpu.VMEM((r, r), F32),
            pltpu.VMEM((m, LANES), F32),
            pltpu.VMEM((r, m), F32),
            pltpu.VMEM((3 * r, m), BF16),
            pltpu.VMEM((m, r), F32),
            *two(len(GATHER), modes), dma((len(GATHER),)), dma((modes + 1,)),
            *two(SLICES, cores), *two(SLICES, modes), *two(SLICES, depth), *two(SLICES, depth),
            *two(SLICES, modes), *two(SLICES, modes, cores),
            *two(cores), *two(depth), *two(modes), *two(modes, cores),
            *two(len(SCATTER), modes),
        ],
        compiler_params=pltpu.CompilerParams(
            collective_id=0, has_side_effects=True, vmem_limit_bytes=48 * 1024 * 1024
        ),
        name="truncate",
    )(unfolded, pltpu.with_memory_space_constraint(start_block, pltpu.HBM))


def emit_kernel(*refs):
    count = len(refs) // 2
    sem = refs[-1]
    copies = [pltpu.make_async_copy(refs[k], refs[count + k], sem.at[k]) for k in range(count)]
    for copy in copies:
        copy.start()
    for copy in copies:
        copy.wait()


def emit(*arrays):
    count = len(arrays)
    return pl.pallas_call(
        emit_kernel,
        out_shape=tuple(jax.ShapeDtypeStruct(x.shape, x.dtype) for x in arrays),
        in_specs=[pl.BlockSpec(memory_space=pl.ANY)] * count,
        out_specs=(pl.BlockSpec(memory_space=pltpu.HBM),) * count,
        scratch_shapes=[pltpu.SemaphoreType.DMA((count,))],
        compiler_params=pltpu.CompilerParams(vmem_limit_bytes=1024 * 1024),
        name="emit",
    )(*arrays)


def per_device(unfolded, start_block):
    return emit(*program(unfolded, start_block, lax.axis_size("mode"), lax.axis_size("rest")))


def solution(mesh):
    return jax.shard_map(
        per_device,
        mesh=mesh,
        in_specs=(P("mode", "rest"), P()),
        out_specs=(P(), P(), P("mode", "rest")),
        check_vma=False,
    )
```

```python
import functools

import jax
import jax.numpy as jnp
from jax import lax
from jax.experimental import pallas as pl
from jax.experimental.pallas import tpu as pltpu
from jax.sharding import PartitionSpec as P

ITERS = 3
SUB = 8
MACRO = 32
MICRO = 16
SLICES = 2
LANES = 128
F32 = jnp.float32
BF16 = jnp.bfloat16
MESH = pl.DeviceIdType.MESH


def parts3(x):
    hi = x.astype(BF16).astype(F32)
    rest = x - hi
    mid = rest.astype(BF16).astype(F32)
    return hi, mid, rest - mid


def nt(x, y):
    return lax.dot_general(x, y, (((1,), (1,)), ((), ())), preferred_element_type=F32)


def nn(x, y):
    return lax.dot_general(x, y, (((1,), (0,)), ((), ())), preferred_element_type=F32)


def dotf(x, y, dims):
    return lax.dot_general(
        x, y, (dims, ((), ())), precision=lax.Precision.HIGHEST, preferred_element_type=F32
    )


def spread(x, row):
    return jnp.broadcast_to(x[row : row + 1, :], x.shape)


def column(x, lane):
    return jnp.broadcast_to(x[:, lane : lane + 1], x.shape)


def invert_block(ref, base, r0):
    tiles = MACRO // SUB
    rows = [ref[pl.ds(base + r0 + SUB * h, SUB), :] for h in range(tiles)]
    lane = lax.broadcasted_iota(jnp.int32, (SUB, LANES), 1)
    sub = lax.broadcasted_iota(jnp.int32, (SUB, LANES), 0)
    pivots = [None] * tiles

    def retire(k, f):
        t, s = divmod(k, SUB)
        here = lane == r0 + k
        row = jnp.where(here, 1.0, spread(rows[t], s))
        for h in range(t, tiles):
            if h == t:
                old = jnp.where(here & (sub >= s), jnp.where(sub == s, 1.0, 0.0), rows[h])
            else:
                old = jnp.where(here, 0.0, rows[h])
            rows[h] = old - f[h] * row

    for first in range(0, MACRO, MICRO):
        stop = first + MICRO
        cols = {(j, h): column(rows[h], r0 + j) for j in range(first, stop) for h in range(j // SUB, tiles)}
        for k in range(first, stop, 2):
            t, s = divmod(k, SUB)
            p = spread(cols[k, t], s)
            a = spread(cols[k, t], s + 1)
            b = spread(cols[k + 1, t], s + 1)
            det = p * b - a * a
            inv_p = 1.0 / p
            inv_q = p * (1.0 / det)
            found = jnp.where(sub == s, p, det * inv_p)
            pivots[t] = found if s == 0 else jnp.where(sub >= s, found, pivots[t])
            f = {h: cols[k, h] * inv_p for h in range(t, tiles)}
            f[t] = jnp.where(sub > s, f[t], 0.0)
            second = {h: cols[k + 1, h] - f[h] * a for h in range(t, tiles)}
            g = {h: second[h] * inv_q for h in range(t, tiles)}
            g[t] = jnp.where(sub > s + 1, g[t], 0.0)
            for j in range(k + 2, stop):
                one = spread(cols[k, j // SUB], j % SUB)
                two = spread(second[j // SUB], j % SUB)
                for h in range(j // SUB, tiles):
                    cols[j, h] = (cols[j, h] - f[h] * one) - g[h] * two
            retire(k, f)
            retire(k + 1, g)
    for h in range(tiles):
        s = lax.rsqrt(pivots[h])
        s = s * (1.5 - 0.5 * pivots[h] * s * s)
        rows[h] = rows[h] * s
        ref[pl.ds(base + r0 + SUB * h, SUB), :] = rows[h]
    size = LANES - r0 - MACRO
    if size == 0:
        return
    lane = lax.broadcasted_iota(jnp.int32, (MACRO, LANES), 1)
    row = lax.broadcasted_iota(jnp.int32, (MACRO, LANES), 0)
    keep = lane >= r0 + MACRO
    lower = keep | (lane <= row + r0)
    pieces = parts3(jnp.concatenate(rows, axis=0))
    lh, lm, ll = (jnp.where(keep, x, 0.0) for x in pieces)
    rh, rm, rl = (jnp.where(lower, x, 0.0) for x in pieces)
    left = jnp.concatenate([lh, lh, lm, lm, lh, ll], axis=0).astype(BF16)
    right = jnp.concatenate([rh, rm, rh, rm, rl, rh], axis=0).astype(BF16)
    upd = lax.dot_general(left, right, (((0,), (0,)), ((), ())), preferred_element_type=F32)
    lane = lax.broadcasted_iota(jnp.int32, (size, LANES), 1)
    inside = (lane >= r0) & (lane < r0 + MACRO)
    spot = pl.ds(base + r0 + MACRO, size)
    ref[spot, :] = jnp.where(inside, 0.0, ref[spot, :]) - upd[r0 + MACRO :, :]


def invert(ref, base):
    for r0 in range(0, LANES, MACRO):
        invert_block(ref, base, r0)


def stack(pieces, axis=0):
    return jnp.concatenate(pieces, axis=axis).astype(BF16)


def invert_scaled(ref, base):
    spot = pl.ds(base, LANES)
    block = ref[spot, :]
    row = lax.broadcasted_iota(jnp.int32, block.shape, 0)
    col = lax.broadcasted_iota(jnp.int32, block.shape, 1)
    diagonal = jnp.where(row == col, block, 0.0)
    below = lax.rsqrt(jnp.sum(diagonal, axis=1, keepdims=True))
    size = jnp.sum(diagonal, axis=0, keepdims=True)
    across = lax.rsqrt(size)
    ref[spot, :] = (block * below) * across
    invert(ref, base)
    ref[spot, :] = ref[spot, :] * jnp.where(row >= col, across, size * across)


def lower_part(x):
    row = lax.broadcasted_iota(jnp.int32, x.shape, 0)
    col = lax.broadcasted_iota(jnp.int32, x.shape, 1)
    return jnp.where(row >= col, x, 0.0)


def cuts(width, weights):
    unit = width // sum(weights)
    starts = [unit * sum(weights[:k]) for k in range(len(weights))]
    return [(start, unit * weight) for start, weight in zip(starts, weights)]


def split(x):
    hi = x.astype(BF16)
    return hi, (x - hi.astype(F32)).astype(BF16)


def off_pairs(count):
    return [(i, j) for i in range(count) for j in range(i + 1, count)]


def owners_of(depth):
    return (depth // 4, depth // 2) if depth % 4 == 0 else (0, depth)


GATHER = (6, 4, 3, 2, 1)
SCATTER = (1, 1, 2, 2, 2)


def kernel(shape, total_cols, x_ref, start_ref, tri_ref, factor_ref, core_ref,
           full, hi_ref, lo_ref, own, part, acc, tot, dacc, dtot, got_c, got_m, got_z, sum1, sum2, dgot_c, dgot_z,
           work, gram_h, gram_m, gram_l, small, panel, basis, pieces_ref, begin,
           row_s, row_r, row_l, own_l, c_s, c_r, m_s, m_r, z_s, z_r, az_s, az_r, am_s, am_r, ac_s, ac_r,
           dc_s, dc_r, dz_s, dz_r, dm_s, dm_r, df_s, df_r, out_s, out_r):
    modes, cores, depth = shape
    me_mode = lax.axis_index("mode")
    me_rest = lax.axis_index("rest")
    me_core = lax.rem(me_rest, cores)
    me_z = me_rest // cores
    first_owner, owners = owners_of(depth)
    is_owner = jnp.logical_and(me_z >= first_owner, me_z < first_owner + owners)
    m, width = full.shape
    rows_dev, cols_dev = x_ref.shape
    rounds = m // LANES

    def mode_peer(off):
        other = lax.rem(me_mode + off, modes)
        return other, (other, me_rest)

    def core_peer(off):
        other = lax.rem(me_core + off, cores)
        return other, (me_mode, me_z * cores + other)

    def z_peer(off):
        other = lax.rem(me_z + off, depth)
        return other, (me_mode, other * cores + me_core)

    def remote(source, target, send, recv, device):
        return pltpu.make_async_remote_copy(
            src_ref=source, dst_ref=target, send_sem=send, recv_sem=recv, device_id=device, device_id_type=MESH
        )

    def at(start, size):
        return pl.ds(pl.multiple_of(start, SUB), size)

    def each_z(body):
        def step(off, carry):
            body(off)
            return carry
        lax.fori_loop(1, depth, step, 0)

    barrier = pltpu.get_barrier_semaphore()
    for peer, size in ((core_peer, cores), (mode_peer, modes)):
        for off in range(1, size):
            pl.semaphore_signal(barrier, inc=1, device_id=peer(off)[1], device_id_type=MESH)
    each_z(lambda off: pl.semaphore_signal(barrier, inc=1, device_id=z_peer(off)[1], device_id_type=MESH))
    pl.semaphore_wait(barrier, modes + cores + depth - 3)

    pieces = cuts(width, GATHER)
    mine_rows = pl.ds(pl.multiple_of(me_mode * rows_dev, rows_dev), rows_dev)
    arrivals = []
    for c, (start, size) in enumerate(pieces):
        spot = (mine_rows, pl.ds(start, size))
        batch = []
        for off in range(1, modes):
            other, device = mode_peer(off)
            batch.append(remote(
                x_ref.at[:, pl.ds(pl.multiple_of(other * width + start, LANES), size)], full.at[spot],
                row_s.at[c, off], row_r.at[c, off], device,
            ))
        batch.append(pltpu.make_async_copy(
            x_ref.at[:, pl.ds(pl.multiple_of(me_mode * width + start, LANES), size)], full.at[spot], row_l.at[c]
        ))
        for copy in batch:
            copy.start()
        arrivals.append(batch)
    loads = []
    for q in range(modes):
        cols = pl.ds(q * width, width)
        load = pltpu.make_async_copy(x_ref.at[:, cols], own.at[:, cols], own_l.at[q])
        load.start()
        loads.append(load)

    fetch = pltpu.make_async_copy(start_ref, begin, own_l.at[modes])
    fetch.start()
    dacc[...] = jnp.zeros_like(dacc)
    acc[...] = jnp.zeros_like(acc)
    for q in range(modes):
        loads[q].wait()
        h, l = split(own[:, pl.ds(q * width, width)])
        cross = nt(h, l)
        dacc[...] += nt(h, h) + (cross + cross.T)
    half = rows_dev // cores
    pending = []
    for off in range(1, cores):
        other, device = core_peer(off)
        copy = remote(dacc.at[at(other * half, half)], dgot_c.at[off - 1], dc_s.at[off], dc_r.at[off], device)
        copy.start()
        pending.append(copy)

    pairs = off_pairs(rounds)

    padded = acc.shape[0]
    h0 = padded // SLICES
    h1 = h0 // cores
    h2 = h1 // modes
    h3 = h2 // owners
    sends = []
    stage_c = []

    def begin_slice(s):
        batch = []
        for off in range(1, cores):
            other, device = core_peer(off)
            copy = remote(acc.at[at(s * h0 + other * h1, h1)], got_c.at[s, off - 1], c_s.at[s, off], c_r.at[s, off], device)
            copy.start()
            batch.append(copy)
        stage_c.append(batch)

    def absorb(c):
        for copy in arrivals[c]:
            copy.wait()
        start, size = pieces[c]
        cols = pl.ds(start, size)
        hi, lo = split(full[:, cols])
        hi_ref[:, cols] = hi
        lo_ref[:, cols] = lo
        for i in range(rounds - 1):
            top = slice(i * LANES, (i + 1) * LANES)
            rest = slice((i + 1) * LANES, m)
            strip = nt(hi[top], hi[rest]) + (nt(hi[top], lo[rest]) + nt(lo[top], hi[rest]))
            for j in range(i + 1, rounds):
                spot = pl.ds(pairs.index((i, j)) * LANES, LANES)
                acc[spot, :] += strip[:, (j - i - 1) * LANES : (j - i) * LANES]
            if c == len(pieces) - 1:
                done = len([p for p in pairs if p[0] <= i]) * LANES
                while (len(stage_c) + 1) * h0 <= done:
                    begin_slice(len(stage_c))

    absorb(0)
    fetch.wait()
    pieces_ref[...] = stack(parts3(begin[...].T))
    for copy in pending:
        copy.wait()
    value = dacc[at(me_core * half, half), :]
    for off in range(1, cores):
        value = value + dgot_c[off - 1]
    dgot_z[me_z] = value

    def dz_copy(off):
        _, device = z_peer(off)
        return remote(dgot_z.at[me_z], dgot_z.at[me_z], dz_s.at[off], dz_r.at[off], device)

    each_z(lambda off: dz_copy(off).start())
    absorb(1)
    each_z(lambda off: dz_copy(off).wait())
    value = lax.fori_loop(1, depth, lambda z, v: v + dgot_z[z], dgot_z[0])
    dmine = at(me_mode * rows_dev + me_core * half, half)
    dtot[dmine, :] = value / total_cols
    for c in range(2, len(pieces)):
        absorb(c)

    for s in range(len(stage_c), SLICES):
        begin_slice(s)
    stage_m = []
    for s in range(SLICES):
        value = acc[at(s * h0 + me_core * h1, h1), :]
        for off, copy in enumerate(stage_c[s]):
            copy.wait_recv()
            value = value + got_c[s, off]
        sends += stage_c[s]
        sum1[s] = value
        batch = []
        for off in range(1, modes):
            other, device = mode_peer(off)
            copy = remote(sum1.at[s, at(other * h2, h2)], got_m.at[s, off - 1], m_s.at[s, off], m_r.at[s, off], device)
            copy.start()
            batch.append(copy)
        stage_m.append(batch)
    stage_d = []
    for off in range(1, modes):
        other, device = mode_peer(off)
        copy = remote(dtot.at[dmine], dtot.at[dmine], dm_s.at[off], dm_r.at[off], device)
        copy.start()
        stage_d.append(copy)

    def forward(relays, ref, spot, send, recv):
        for off in range(1, cores):
            _, device = core_peer(off)
            copy = remote(ref.at[spot], ref.at[spot], send.at[off], recv.at[off], device)
            copy.start()
            sends.append(copy)
            relays.append(copy)

    relays = []

    def keep_gram(spot, piece):
        for ref, value in zip((gram_h, gram_m, gram_l), parts3(piece)):
            ref[spot] = value.astype(BF16)

    forward(relays, dtot, dmine, df_s.at[0], df_r.at[0])

    def z_copy(s, off):
        other, device = z_peer(off)
        return remote(
            sum2.at[s, at(jnp.clip(other - first_owner, 0, owners - 1) * h3, h3)], got_z.at[s, off],
            z_s.at[s, off], z_r.at[s, off], device,
        )

    def owned(z):
        return jnp.logical_and(z >= first_owner, z < first_owner + owners)

    def to_owner(off, act):
        pl.when(owned(z_peer(off)[0]))(act)

    for s in range(SLICES):
        value = sum1[s, at(me_mode * h2, h2), :]
        for off, copy in enumerate(stage_m[s]):
            copy.wait_recv()
            value = value + got_m[s, off]
        sends += stage_m[s]
        sum2[s] = value
        each_z(lambda off: to_owner(off, lambda: z_copy(s, off).start()))

    def my_start(s):
        return s * h0 + me_core * h1 + me_mode * h2

    def az_copy(s, off, z):
        _, device = z_peer(off)
        block = tot.at[at(my_start(s) + jnp.clip(z - first_owner, 0, owners - 1) * h3, h3)]
        return remote(block, block, az_s.at[s, off], az_r.at[s, off], device)

    for s in range(SLICES):
        @pl.when(is_owner)
        def _():
            each_z(lambda off: z_copy(s, off).wait_recv())
            spot = at(jnp.clip(me_z - first_owner, 0, owners - 1) * h3, h3)
            value = lax.fori_loop(1, depth, lambda off, v: v + got_z[s, off], sum2[s, spot, :])
            tot[at(my_start(s) + jnp.clip(me_z - first_owner, 0, owners - 1) * h3, h3), :] = value / total_cols
            each_z(lambda off: az_copy(s, off, me_z).start())

    for off, copy in enumerate(stage_d, 1):
        copy.wait_recv()
        source = lax.rem(me_mode - off + modes, modes)
        forward(relays, dtot, at(source * rows_dev + me_core * half, half), df_s.at[off], df_r.at[off])
    sends += stage_d
    for copy in relays:
        copy.wait_recv()
    for i in range(rounds):
        spot = (pl.ds(i * LANES, LANES), pl.ds(i * LANES, LANES))
        piece = dtot[pl.ds(i * LANES, LANES), :]
        keep_gram(spot, piece)
        work[spot] = piece
    panel[pl.ds(0, LANES), :] = dtot[pl.ds(0, LANES), :]
    invert_scaled(panel, 0)

    stage_a = []
    hops = []
    for s in range(SLICES):
        def arrive(off):
            source = lax.rem(me_z - off + depth, depth)
            pl.when(owned(source))(lambda: az_copy(s, off, source).wait_recv())
        each_z(arrive)
        block = at(my_start(s), h2)
        batch = []
        for off in range(1, modes):
            other, device = mode_peer(off)
            copy = remote(tot.at[block], tot.at[block], am_s.at[s, off], am_r.at[s, off], device)
            copy.start()
            batch.append(copy)
        hops.append([])
        forward(hops[s], tot, block, ac_s.at[s, 0], ac_r.at[s, 0])
        stage_a.append(batch)
    for s in range(SLICES):
        for off, copy in enumerate(stage_a[s], 1):
            copy.wait_recv()
            source = lax.rem(me_mode - off + modes, modes)
            forward(hops[s], tot, at(s * h0 + me_core * h1 + source * h2, h2), ac_s.at[s, off], ac_r.at[s, off])
        sends += stage_a[s]
    for s in range(SLICES):
        for copy in hops[s]:
            copy.wait_recv()
        for where, (i, j) in enumerate(pairs):
            if (where * LANES + LANES - 1) // h0 == s:
                piece = tot[pl.ds(where * LANES, LANES), :]
                spot = (pl.ds(i * LANES, LANES), pl.ds(j * LANES, LANES))
                work[spot] = piece
                keep_gram(spot, piece)
                keep_gram(spot[::-1], piece.T)

    r = basis.shape[0]

    def iterate(t, carry):
        old = pieces_ref[...]
        one = nn(old, gram_h[...])
        two = nn(old[: 2 * r], gram_m[...])
        image = one[:r] + ((one[r : 2 * r] + two[:r]) + (one[2 * r :] + (two[r:] + nn(old[:r], gram_l[...]))))
        image = image * lax.rsqrt(jnp.sum(image * image, axis=1, keepdims=True))
        ih, im, il = parts3(image)
        new = stack([ih, im, il])
        q = nt(new, new[: 2 * r])
        low = q[2 * r :, :r]
        small[...] = q[:r, :r] + ((q[:r, r:] + q[r : 2 * r, :r]) + (q[r : 2 * r, r:] + (low + low.T)))
        invert(small, 0)
        wh, wm, wl = parts3(lower_part(small[...]))
        high = nn(stack([stack([wh, wh], 1), stack([wm, wm], 1)]), new[: 2 * r])
        rest = nn(stack([wl, wh], 1), stack([ih, il]))
        result = high[:r] + (high[r:] + rest)
        basis[...] = result
        pieces_ref[...] = stack(parts3(result))
        return carry

    lax.fori_loop(0, ITERS, iterate, 0)
    basis_t = basis[...]
    bh, bl = pieces_ref[:r, :], pieces_ref[r : 2 * r, :]
    out_rows = core_ref.shape[0]
    for c, (start, size) in enumerate(cuts(width, SCATTER)):
        cols = pl.ds(start, size)
        xh = hi_ref[:, cols]
        part[:, cols] = nn(bh, xh) + (nn(bh, lo_ref[:, cols]) + nn(bl, xh))
        mine = pl.ds(pl.multiple_of(me_mode * width + start, LANES), size)
        for off in range(1, modes):
            other, device = mode_peer(off)
            copy = remote(
                part.at[at(other * out_rows, out_rows), cols], core_ref.at[:, mine], out_s.at[c, off], out_r.at[c, off], device
            )
            copy.start()
            sends.append(copy)
            arrivals.append([copy])
        core_ref[:, mine] = part[at(me_mode * out_rows, out_rows), cols]
    factor_ref[...] = basis_t.T

    for t in range(rounds):
        base = t * LANES
        here = pl.ds(base, LANES)
        if t > 0:
            panel[here, :] = work[here, here]
            invert_scaled(panel, base)
        if t < rounds - 1:
            tail = pl.ds(base + LANES, m - base - LANES)
            u = dotf(lower_part(panel[here, :]), work[here, tail], ((1,), (0,)))
            work[here, tail] = u
            work[tail, tail] -= dotf(u, u, ((0,), (0,)))
    row = lax.broadcasted_iota(jnp.int32, (LANES, LANES), 0)
    col = lax.broadcasted_iota(jnp.int32, (LANES, LANES), 1)
    for i in range(rounds):
        for j in range(rounds):
            spot = (pl.ds(j * LANES, LANES), pl.ds(i * LANES, LANES))
            if j < i:
                tri_ref[spot] = jnp.zeros((LANES, LANES), F32)
            elif j > i:
                tri_ref[spot] = work[spot[::-1]].T
            else:
                piece = panel[pl.ds(i * LANES, LANES), :]
                tri_ref[spot] = jnp.where(row < col, piece, jnp.where(row == col, 1.0 / piece, 0.0)).T

    for copy in sends:
        copy.wait_send()
    for s in range(SLICES):
        each_z(lambda off: to_owner(off, lambda: z_copy(s, off).wait_send()))

        @pl.when(is_owner)
        def _():
            each_z(lambda off: az_copy(s, off, me_z).wait_send())
    for batch in arrivals[len(pieces):]:
        for copy in batch:
            copy.wait_recv()


def program(unfolded, start_block, modes, rest):
    rows_dev, cols_dev = unfolded.shape
    m, r = start_block.shape
    width = cols_dev // modes
    cores = 2 if rest % 2 == 0 else 1
    depth = rest // cores
    owners = owners_of(depth)[1]
    unit = SLICES * cores * modes * owners * SUB
    padded = pl.cdiv(len(off_pairs(m // LANES)) * LANES, unit) * unit
    h1 = padded // SLICES // cores
    h2 = h1 // modes
    h3 = h2 // owners
    half = rows_dev // cores
    vmem = pl.BlockSpec(memory_space=pltpu.VMEM)
    dma = pltpu.SemaphoreType.DMA
    few = max(cores - 1, 1)
    two = lambda *shape: [dma(shape), dma(shape)]
    return pl.pallas_call(
        functools.partial(kernel, (modes, cores, depth), cols_dev * rest),
        out_shape=(
            jax.ShapeDtypeStruct((m, m), F32),
            jax.ShapeDtypeStruct((m, r), F32),
            jax.ShapeDtypeStruct((r // modes, cols_dev), F32),
        ),
        in_specs=[pl.BlockSpec(memory_space=pltpu.HBM)] * 2,
        out_specs=(vmem, vmem, vmem),
        scratch_shapes=[
            pltpu.VMEM((m, width), F32),
            pltpu.VMEM((m, width), BF16),
            pltpu.VMEM((m, width), BF16),
            pltpu.VMEM((rows_dev, cols_dev), F32),
            pltpu.VMEM((r, width), F32),
            pltpu.VMEM((padded, LANES), F32),
            pltpu.VMEM((padded, LANES), F32),
            pltpu.VMEM((rows_dev, rows_dev), F32),
            pltpu.VMEM((m, LANES), F32),
            pltpu.VMEM((SLICES, few, h1, LANES), F32),
            pltpu.VMEM((SLICES, modes, h2, LANES), F32),
            pltpu.VMEM((SLICES, depth, h3, LANES), F32),
            pltpu.VMEM((SLICES, h1, LANES), F32),
            pltpu.VMEM((SLICES, h2, LANES), F32),
            pltpu.VMEM((few, half, LANES), F32),
            pltpu.VMEM((depth, half, LANES), F32),
            pltpu.VMEM((m, m), F32),
            *[pltpu.VMEM((m, m), BF16)] * 3,
            pltpu.VMEM((r, r), F32),
            pltpu.VMEM((m, LANES), F32),
            pltpu.VMEM((r, m), F32),
            pltpu.VMEM((3 * r, m), BF16),
            pltpu.VMEM((m, r), F32),
            *two(len(GATHER), modes), dma((len(GATHER),)), dma((modes + 1,)),
            *two(SLICES, cores), *two(SLICES, modes), *two(SLICES, depth), *two(SLICES, depth),
            *two(SLICES, modes), *two(SLICES, modes, cores),
            *two(cores), *two(depth), *two(modes), *two(modes, cores),
            *two(len(SCATTER), modes),
        ],
        compiler_params=pltpu.CompilerParams(
            collective_id=0, has_side_effects=True, vmem_limit_bytes=48 * 1024 * 1024
        ),
        name="truncate",
    )(unfolded, pltpu.with_memory_space_constraint(start_block, pltpu.HBM))


def emit_kernel(*refs):
    count = len(refs) // 2
    sem = refs[-1]
    copies = [pltpu.make_async_copy(refs[k], refs[count + k], sem.at[k]) for k in range(count)]
    for copy in copies:
        copy.start()
    for copy in copies:
        copy.wait()


def emit(*arrays):
    count = len(arrays)
    return pl.pallas_call(
        emit_kernel,
        out_shape=tuple(jax.ShapeDtypeStruct(x.shape, x.dtype) for x in arrays),
        in_specs=[pl.BlockSpec(memory_space=pl.ANY)] * count,
        out_specs=(pl.BlockSpec(memory_space=pltpu.HBM),) * count,
        scratch_shapes=[pltpu.SemaphoreType.DMA((count,))],
        compiler_params=pltpu.CompilerParams(vmem_limit_bytes=1024 * 1024),
        name="emit",
    )(*arrays)


def per_device(unfolded, start_block):
    return emit(*program(unfolded, start_block, lax.axis_size("mode"), lax.axis_size("rest")))


def solution(mesh):
    return jax.shard_map(
        per_device,
        mesh=mesh,
        in_specs=(P("mode", "rest"), P()),
        out_specs=(P(), P(), P("mode", "rest")),
        check_vma=False,
    )
```

```python
import functools

import jax
import jax.numpy as jnp
from jax import lax
from jax.experimental import pallas as pl
from jax.experimental.pallas import tpu as pltpu
from jax.sharding import PartitionSpec as P

ITERS = 3
SUB = 8
MACRO = 32
MICRO = 16
SLICES = 2
LANES = 128
F32 = jnp.float32
BF16 = jnp.bfloat16
MESH = pl.DeviceIdType.MESH


def parts3(x):
    hi = x.astype(BF16).astype(F32)
    rest = x - hi
    mid = rest.astype(BF16).astype(F32)
    return hi, mid, rest - mid


def nt(x, y):
    return lax.dot_general(x, y, (((1,), (1,)), ((), ())), preferred_element_type=F32)


def nn(x, y):
    return lax.dot_general(x, y, (((1,), (0,)), ((), ())), preferred_element_type=F32)


def dotf(x, y, dims):
    return lax.dot_general(
        x, y, (dims, ((), ())), precision=lax.Precision.HIGHEST, preferred_element_type=F32
    )


def spread(x, row):
    return jnp.broadcast_to(x[row : row + 1, :], x.shape)


def column(x, lane):
    return jnp.broadcast_to(x[:, lane : lane + 1], x.shape)


def invert_block(ref, base, r0):
    tiles = MACRO // SUB
    rows = [ref[pl.ds(base + r0 + SUB * h, SUB), :] for h in range(tiles)]
    lane = lax.broadcasted_iota(jnp.int32, (SUB, LANES), 1)
    sub = lax.broadcasted_iota(jnp.int32, (SUB, LANES), 0)
    pivots = [None] * tiles

    def retire(k, f):
        t, s = divmod(k, SUB)
        here = lane == r0 + k
        row = jnp.where(here, 1.0, spread(rows[t], s))
        for h in range(t, tiles):
            if h == t:
                old = jnp.where(here & (sub >= s), jnp.where(sub == s, 1.0, 0.0), rows[h])
            else:
                old = jnp.where(here, 0.0, rows[h])
            rows[h] = old - f[h] * row

    for first in range(0, MACRO, MICRO):
        stop = first + MICRO
        cols = {(j, h): column(rows[h], r0 + j) for j in range(first, stop) for h in range(j // SUB, tiles)}
        for k in range(first, stop, 2):
            t, s = divmod(k, SUB)
            p = spread(cols[k, t], s)
            a = spread(cols[k, t], s + 1)
            b = spread(cols[k + 1, t], s + 1)
            det = p * b - a * a
            inv_p = 1.0 / p
            inv_q = p * (1.0 / det)
            found = jnp.where(sub == s, p, det * inv_p)
            pivots[t] = found if s == 0 else jnp.where(sub >= s, found, pivots[t])
            f = {h: cols[k, h] * inv_p for h in range(t, tiles)}
            f[t] = jnp.where(sub > s, f[t], 0.0)
            second = {h: cols[k + 1, h] - f[h] * a for h in range(t, tiles)}
            g = {h: second[h] * inv_q for h in range(t, tiles)}
            g[t] = jnp.where(sub > s + 1, g[t], 0.0)
            for j in range(k + 2, stop):
                one = spread(cols[k, j // SUB], j % SUB)
                two = spread(second[j // SUB], j % SUB)
                for h in range(j // SUB, tiles):
                    cols[j, h] = (cols[j, h] - f[h] * one) - g[h] * two
            retire(k, f)
            retire(k + 1, g)
    for h in range(tiles):
        s = lax.rsqrt(pivots[h])
        s = s * (1.5 - 0.5 * pivots[h] * s * s)
        rows[h] = rows[h] * s
        ref[pl.ds(base + r0 + SUB * h, SUB), :] = rows[h]
    size = LANES - r0 - MACRO
    if size == 0:
        return
    lane = lax.broadcasted_iota(jnp.int32, (MACRO, LANES), 1)
    row = lax.broadcasted_iota(jnp.int32, (MACRO, LANES), 0)
    keep = lane >= r0 + MACRO
    lower = keep | (lane <= row + r0)
    pieces = parts3(jnp.concatenate(rows, axis=0))
    lh, lm, ll = (jnp.where(keep, x, 0.0) for x in pieces)
    rh, rm, rl = (jnp.where(lower, x, 0.0) for x in pieces)
    left = jnp.concatenate([lh, lh, lm, lm, lh, ll], axis=0).astype(BF16)
    right = jnp.concatenate([rh, rm, rh, rm, rl, rh], axis=0).astype(BF16)
    upd = lax.dot_general(left, right, (((0,), (0,)), ((), ())), preferred_element_type=F32)
    lane = lax.broadcasted_iota(jnp.int32, (size, LANES), 1)
    inside = (lane >= r0) & (lane < r0 + MACRO)
    spot = pl.ds(base + r0 + MACRO, size)
    ref[spot, :] = jnp.where(inside, 0.0, ref[spot, :]) - upd[r0 + MACRO :, :]


def invert(ref, base):
    for r0 in range(0, LANES, MACRO):
        invert_block(ref, base, r0)


def stack(pieces, axis=0):
    return jnp.concatenate(pieces, axis=axis).astype(BF16)


def invert_scaled(ref, base):
    spot = pl.ds(base, LANES)
    block = ref[spot, :]
    row = lax.broadcasted_iota(jnp.int32, block.shape, 0)
    col = lax.broadcasted_iota(jnp.int32, block.shape, 1)
    diagonal = jnp.where(row == col, block, 0.0)
    below = lax.rsqrt(jnp.sum(diagonal, axis=1, keepdims=True))
    size = jnp.sum(diagonal, axis=0, keepdims=True)
    across = lax.rsqrt(size)
    ref[spot, :] = (block * below) * across
    invert(ref, base)
    ref[spot, :] = ref[spot, :] * jnp.where(row >= col, across, size * across)


def lower_part(x):
    row = lax.broadcasted_iota(jnp.int32, x.shape, 0)
    col = lax.broadcasted_iota(jnp.int32, x.shape, 1)
    return jnp.where(row >= col, x, 0.0)


def cuts(width, weights):
    unit = width // sum(weights)
    starts = [unit * sum(weights[:k]) for k in range(len(weights))]
    return [(start, unit * weight) for start, weight in zip(starts, weights)]


def split(x):
    hi = x.astype(BF16)
    return hi, (x - hi.astype(F32)).astype(BF16)


def off_pairs(count):
    return [(i, j) for i in range(count) for j in range(i + 1, count)]


def owners_of(depth):
    return (depth // 4, depth // 2) if depth % 4 == 0 else (0, depth)


GATHER = (6, 4, 3, 2, 1)
SCATTER = (1, 1, 2, 2, 2)


def kernel(shape, total_cols, x_ref, start_ref, tri_ref, factor_ref, core_ref,
           full, hi_ref, lo_ref, own, part, acc, tot, dacc, dtot, got_c, got_m, got_z, sum1, sum2, dgot_c, dgot_z,
           work, gram_h, gram_m, gram_l, small, panel, basis, pieces_ref, begin,
           row_s, row_r, row_l, own_l, c_s, c_r, m_s, m_r, z_s, z_r, az_s, az_r, am_s, am_r, ac_s, ac_r,
           dc_s, dc_r, dz_s, dz_r, dm_s, dm_r, df_s, df_r, out_s, out_r):
    modes, cores, depth = shape
    me_mode = lax.axis_index("mode")
    me_rest = lax.axis_index("rest")
    me_core = lax.rem(me_rest, cores)
    me_z = me_rest // cores
    first_owner, owners = owners_of(depth)
    is_owner = jnp.logical_and(me_z >= first_owner, me_z < first_owner + owners)
    m, width = full.shape
    rows_dev, cols_dev = x_ref.shape
    rounds = m // LANES

    def mode_peer(off):
        other = lax.rem(me_mode + off, modes)
        return other, (other, me_rest)

    def core_peer(off):
        other = lax.rem(me_core + off, cores)
        return other, (me_mode, me_z * cores + other)

    def z_peer(off):
        other = lax.rem(me_z + off, depth)
        return other, (me_mode, other * cores + me_core)

    def remote(source, target, send, recv, device):
        return pltpu.make_async_remote_copy(
            src_ref=source, dst_ref=target, send_sem=send, recv_sem=recv, device_id=device, device_id_type=MESH
        )

    def at(start, size):
        return pl.ds(pl.multiple_of(start, SUB), size)

    def each_z(body):
        def step(off, carry):
            body(off)
            return carry
        lax.fori_loop(1, depth, step, 0)

    barrier = pltpu.get_barrier_semaphore()
    for peer, size in ((core_peer, cores), (mode_peer, modes)):
        for off in range(1, size):
            pl.semaphore_signal(barrier, inc=1, device_id=peer(off)[1], device_id_type=MESH)
    each_z(lambda off: pl.semaphore_signal(barrier, inc=1, device_id=z_peer(off)[1], device_id_type=MESH))
    pl.semaphore_wait(barrier, modes + cores + depth - 3)

    pieces = cuts(width, GATHER)
    mine_rows = pl.ds(pl.multiple_of(me_mode * rows_dev, rows_dev), rows_dev)
    arrivals = []
    for c, (start, size) in enumerate(pieces):
        spot = (mine_rows, pl.ds(start, size))
        batch = []
        for off in range(1, modes):
            other, device = mode_peer(off)
            batch.append(remote(
                x_ref.at[:, pl.ds(pl.multiple_of(other * width + start, LANES), size)], full.at[spot],
                row_s.at[c, off], row_r.at[c, off], device,
            ))
        batch.append(pltpu.make_async_copy(
            x_ref.at[:, pl.ds(pl.multiple_of(me_mode * width + start, LANES), size)], full.at[spot], row_l.at[c]
        ))
        for copy in batch:
            copy.start()
        arrivals.append(batch)
    loads = []
    for q in range(modes):
        cols = pl.ds(q * width, width)
        load = pltpu.make_async_copy(x_ref.at[:, cols], own.at[:, cols], own_l.at[q])
        load.start()
        loads.append(load)

    fetch = pltpu.make_async_copy(start_ref, begin, own_l.at[modes])
    fetch.start()
    dacc[...] = jnp.zeros_like(dacc)
    acc[...] = jnp.zeros_like(acc)
    for q in range(modes):
        loads[q].wait()
        h, l = split(own[:, pl.ds(q * width, width)])
        cross = nt(h, l)
        dacc[...] += nt(h, h) + (cross + cross.T)
    half = rows_dev // cores
    pending = []
    for off in range(1, cores):
        other, device = core_peer(off)
        copy = remote(dacc.at[at(other * half, half)], dgot_c.at[off - 1], dc_s.at[off], dc_r.at[off], device)
        copy.start()
        pending.append(copy)

    pairs = off_pairs(rounds)

    padded = acc.shape[0]
    h0 = padded // SLICES
    h1 = h0 // cores
    h2 = h1 // modes
    h3 = h2 // owners
    sends = []
    stage_c = []

    def begin_slice(s):
        batch = []
        for off in range(1, cores):
            other, device = core_peer(off)
            copy = remote(acc.at[at(s * h0 + other * h1, h1)], got_c.at[s, off - 1], c_s.at[s, off], c_r.at[s, off], device)
            copy.start()
            batch.append(copy)
        stage_c.append(batch)

    def absorb(c):
        for copy in arrivals[c]:
            copy.wait()
        start, size = pieces[c]
        cols = pl.ds(start, size)
        hi, lo = split(full[:, cols])
        hi_ref[:, cols] = hi
        lo_ref[:, cols] = lo
        for i in range(rounds - 1):
            top = slice(i * LANES, (i + 1) * LANES)
            rest = slice((i + 1) * LANES, m)
            strip = nt(hi[top], hi[rest]) + (nt(hi[top], lo[rest]) + nt(lo[top], hi[rest]))
            for j in range(i + 1, rounds):
                spot = pl.ds(pairs.index((i, j)) * LANES, LANES)
                acc[spot, :] += strip[:, (j - i - 1) * LANES : (j - i) * LANES]
            if c == len(pieces) - 1:
                done = len([p for p in pairs if p[0] <= i]) * LANES
                while (len(stage_c) + 1) * h0 <= done:
                    begin_slice(len(stage_c))

    absorb(0)
    fetch.wait()
    pieces_ref[...] = stack(parts3(begin[...].T))
    for copy in pending:
        copy.wait()
    value = dacc[at(me_core * half, half), :]
    for off in range(1, cores):
        value = value + dgot_c[off - 1]
    dgot_z[me_z] = value

    def dz_copy(off):
        _, device = z_peer(off)
        return remote(dgot_z.at[me_z], dgot_z.at[me_z], dz_s.at[off], dz_r.at[off], device)

    each_z(lambda off: dz_copy(off).start())
    absorb(1)
    each_z(lambda off: dz_copy(off).wait())
    value = lax.fori_loop(1, depth, lambda z, v: v + dgot_z[z], dgot_z[0])
    dmine = at(me_mode * rows_dev + me_core * half, half)
    dtot[dmine, :] = value / total_cols
    for c in range(2, len(pieces)):
        absorb(c)

    for s in range(len(stage_c), SLICES):
        begin_slice(s)
    stage_m = []
    for s in range(SLICES):
        value = acc[at(s * h0 + me_core * h1, h1), :]
        for off, copy in enumerate(stage_c[s]):
            copy.wait_recv()
            value = value + got_c[s, off]
        sends += stage_c[s]
        sum1[s] = value
        batch = []
        for off in range(1, modes):
            other, device = mode_peer(off)
            copy = remote(sum1.at[s, at(other * h2, h2)], got_m.at[s, off - 1], m_s.at[s, off], m_r.at[s, off], device)
            copy.start()
            batch.append(copy)
        stage_m.append(batch)
    stage_d = []
    for off in range(1, modes):
        other, device = mode_peer(off)
        copy = remote(dtot.at[dmine], dtot.at[dmine], dm_s.at[off], dm_r.at[off], device)
        copy.start()
        stage_d.append(copy)

    def forward(relays, ref, spot, send, recv):
        for off in range(1, cores):
            _, device = core_peer(off)
            copy = remote(ref.at[spot], ref.at[spot], send.at[off], recv.at[off], device)
            copy.start()
            sends.append(copy)
            relays.append(copy)

    relays = []

    def keep_gram(spot, piece):
        for ref, value in zip((gram_h, gram_m, gram_l), parts3(piece)):
            ref[spot] = value.astype(BF16)

    forward(relays, dtot, dmine, df_s.at[0], df_r.at[0])

    def z_copy(s, off):
        other, device = z_peer(off)
        return remote(
            sum2.at[s, at(jnp.clip(other - first_owner, 0, owners - 1) * h3, h3)], got_z.at[s, off],
            z_s.at[s, off], z_r.at[s, off], device,
        )

    def owned(z):
        return jnp.logical_and(z >= first_owner, z < first_owner + owners)

    def to_owner(off, act):
        pl.when(owned(z_peer(off)[0]))(act)

    for s in range(SLICES):
        value = sum1[s, at(me_mode * h2, h2), :]
        for off, copy in enumerate(stage_m[s]):
            copy.wait_recv()
            value = value + got_m[s, off]
        sends += stage_m[s]
        sum2[s] = value
        each_z(lambda off: to_owner(off, lambda: z_copy(s, off).start()))

    def my_start(s):
        return s * h0 + me_core * h1 + me_mode * h2

    def az_copy(s, off, z):
        _, device = z_peer(off)
        block = tot.at[at(my_start(s) + jnp.clip(z - first_owner, 0, owners - 1) * h3, h3)]
        return remote(block, block, az_s.at[s, off], az_r.at[s, off], device)

    for s in range(SLICES):
        @pl.when(is_owner)
        def _():
            each_z(lambda off: z_copy(s, off).wait_recv())
            spot = at(jnp.clip(me_z - first_owner, 0, owners - 1) * h3, h3)
            value = lax.fori_loop(1, depth, lambda off, v: v + got_z[s, off], sum2[s, spot, :])
            tot[at(my_start(s) + jnp.clip(me_z - first_owner, 0, owners - 1) * h3, h3), :] = value / total_cols
            each_z(lambda off: az_copy(s, off, me_z).start())

    for off, copy in enumerate(stage_d, 1):
        copy.wait_recv()
        source = lax.rem(me_mode - off + modes, modes)
        forward(relays, dtot, at(source * rows_dev + me_core * half, half), df_s.at[off], df_r.at[off])
    sends += stage_d
    for copy in relays:
        copy.wait_recv()
    for i in range(rounds):
        spot = (pl.ds(i * LANES, LANES), pl.ds(i * LANES, LANES))
        piece = dtot[pl.ds(i * LANES, LANES), :]
        keep_gram(spot, piece)
        work[spot] = piece
    panel[pl.ds(0, LANES), :] = dtot[pl.ds(0, LANES), :]
    invert_scaled(panel, 0)

    stage_a = []
    hops = []
    for s in range(SLICES):
        def arrive(off):
            source = lax.rem(me_z - off + depth, depth)
            pl.when(owned(source))(lambda: az_copy(s, off, source).wait_recv())
        each_z(arrive)
        block = at(my_start(s), h2)
        batch = []
        for off in range(1, modes):
            other, device = mode_peer(off)
            copy = remote(tot.at[block], tot.at[block], am_s.at[s, off], am_r.at[s, off], device)
            copy.start()
            batch.append(copy)
        hops.append([])
        forward(hops[s], tot, block, ac_s.at[s, 0], ac_r.at[s, 0])
        stage_a.append(batch)
    for s in range(SLICES):
        for off, copy in enumerate(stage_a[s], 1):
            copy.wait_recv()
            source = lax.rem(me_mode - off + modes, modes)
            forward(hops[s], tot, at(s * h0 + me_core * h1 + source * h2, h2), ac_s.at[s, off], ac_r.at[s, off])
        sends += stage_a[s]
    for s in range(SLICES):
        for copy in hops[s]:
            copy.wait_recv()
        for where, (i, j) in enumerate(pairs):
            if (where * LANES + LANES - 1) // h0 == s:
                piece = tot[pl.ds(where * LANES, LANES), :]
                spot = (pl.ds(i * LANES, LANES), pl.ds(j * LANES, LANES))
                work[spot] = piece
                keep_gram(spot, piece)
                keep_gram(spot[::-1], piece.T)

    r = basis.shape[0]

    def iterate(t, carry):
        old = pieces_ref[...]
        one = nn(old, gram_h[...])
        two = nn(old[: 2 * r], gram_m[...])
        image = one[:r] + ((one[r : 2 * r] + two[:r]) + (one[2 * r :] + (two[r:] + nn(old[:r], gram_l[...]))))
        below = lax.rsqrt(jnp.sum(image * image, axis=1, keepdims=True))
        ih, im, il = parts3(image)
        new = stack([ih, im, il])
        q = nt(new, new[: 2 * r])
        low = q[2 * r :, :r]
        gram = q[:r, :r] + ((q[:r, r:] + q[r : 2 * r, :r]) + (q[r : 2 * r, r:] + (low + low.T)))
        row = lax.broadcasted_iota(jnp.int32, (r, r), 0)
        col = lax.broadcasted_iota(jnp.int32, (r, r), 1)
        across = lax.rsqrt(jnp.sum(jnp.where(row == col, gram, 0.0), axis=0, keepdims=True))
        small[...] = (gram * below) * across
        invert(small, 0)
        wh, wm, wl = parts3(lower_part(small[...]) * across)
        high = nn(stack([stack([wh, wh], 1), stack([wm, wm], 1)]), new[: 2 * r])
        rest = nn(stack([wl, wh], 1), stack([ih, il]))
        result = high[:r] + (high[r:] + rest)
        basis[...] = result
        pieces_ref[...] = stack(parts3(result))
        return carry

    lax.fori_loop(0, ITERS, iterate, 0)
    basis_t = basis[...]
    bh, bl = pieces_ref[:r, :], pieces_ref[r : 2 * r, :]
    out_rows = core_ref.shape[0]
    for c, (start, size) in enumerate(cuts(width, SCATTER)):
        cols = pl.ds(start, size)
        xh = hi_ref[:, cols]
        part[:, cols] = nn(bh, xh) + (nn(bh, lo_ref[:, cols]) + nn(bl, xh))
        mine = pl.ds(pl.multiple_of(me_mode * width + start, LANES), size)
        for off in range(1, modes):
            other, device = mode_peer(off)
            copy = remote(
                part.at[at(other * out_rows, out_rows), cols], core_ref.at[:, mine], out_s.at[c, off], out_r.at[c, off], device
            )
            copy.start()
            sends.append(copy)
            arrivals.append([copy])
        core_ref[:, mine] = part[at(me_mode * out_rows, out_rows), cols]
    factor_ref[...] = basis_t.T

    for t in range(rounds):
        base = t * LANES
        here = pl.ds(base, LANES)
        if t > 0:
            panel[here, :] = work[here, here]
            invert_scaled(panel, base)
        if t < rounds - 1:
            tail = pl.ds(base + LANES, m - base - LANES)
            u = dotf(lower_part(panel[here, :]), work[here, tail], ((1,), (0,)))
            work[here, tail] = u
            work[tail, tail] -= dotf(u, u, ((0,), (0,)))
    row = lax.broadcasted_iota(jnp.int32, (LANES, LANES), 0)
    col = lax.broadcasted_iota(jnp.int32, (LANES, LANES), 1)
    for i in range(rounds):
        for j in range(rounds):
            spot = (pl.ds(j * LANES, LANES), pl.ds(i * LANES, LANES))
            if j < i:
                tri_ref[spot] = jnp.zeros((LANES, LANES), F32)
            elif j > i:
                tri_ref[spot] = work[spot[::-1]].T
            else:
                piece = panel[pl.ds(i * LANES, LANES), :]
                tri_ref[spot] = jnp.where(row < col, piece, jnp.where(row == col, 1.0 / piece, 0.0)).T

    for copy in sends:
        copy.wait_send()
    for s in range(SLICES):
        each_z(lambda off: to_owner(off, lambda: z_copy(s, off).wait_send()))

        @pl.when(is_owner)
        def _():
            each_z(lambda off: az_copy(s, off, me_z).wait_send())
    for batch in arrivals[len(pieces):]:
        for copy in batch:
            copy.wait_recv()


def program(unfolded, start_block, modes, rest):
    rows_dev, cols_dev = unfolded.shape
    m, r = start_block.shape
    width = cols_dev // modes
    cores = 2 if rest % 2 == 0 else 1
    depth = rest // cores
    owners = owners_of(depth)[1]
    unit = SLICES * cores * modes * owners * SUB
    padded = pl.cdiv(len(off_pairs(m // LANES)) * LANES, unit) * unit
    h1 = padded // SLICES // cores
    h2 = h1 // modes
    h3 = h2 // owners
    half = rows_dev // cores
    vmem = pl.BlockSpec(memory_space=pltpu.VMEM)
    dma = pltpu.SemaphoreType.DMA
    few = max(cores - 1, 1)
    two = lambda *shape: [dma(shape), dma(shape)]
    return pl.pallas_call(
        functools.partial(kernel, (modes, cores, depth), cols_dev * rest),
        out_shape=(
            jax.ShapeDtypeStruct((m, m), F32),
            jax.ShapeDtypeStruct((m, r), F32),
            jax.ShapeDtypeStruct((r // modes, cols_dev), F32),
        ),
        in_specs=[pl.BlockSpec(memory_space=pltpu.HBM)] * 2,
        out_specs=(vmem, vmem, vmem),
        scratch_shapes=[
            pltpu.VMEM((m, width), F32),
            pltpu.VMEM((m, width), BF16),
            pltpu.VMEM((m, width), BF16),
            pltpu.VMEM((rows_dev, cols_dev), F32),
            pltpu.VMEM((r, width), F32),
            pltpu.VMEM((padded, LANES), F32),
            pltpu.VMEM((padded, LANES), F32),
            pltpu.VMEM((rows_dev, rows_dev), F32),
            pltpu.VMEM((m, LANES), F32),
            pltpu.VMEM((SLICES, few, h1, LANES), F32),
            pltpu.VMEM((SLICES, modes, h2, LANES), F32),
            pltpu.VMEM((SLICES, depth, h3, LANES), F32),
            pltpu.VMEM((SLICES, h1, LANES), F32),
            pltpu.VMEM((SLICES, h2, LANES), F32),
            pltpu.VMEM((few, half, LANES), F32),
            pltpu.VMEM((depth, half, LANES), F32),
            pltpu.VMEM((m, m), F32),
            *[pltpu.VMEM((m, m), BF16)] * 3,
            pltpu.VMEM((r, r), F32),
            pltpu.VMEM((m, LANES), F32),
            pltpu.VMEM((r, m), F32),
            pltpu.VMEM((3 * r, m), BF16),
            pltpu.VMEM((m, r), F32),
            *two(len(GATHER), modes), dma((len(GATHER),)), dma((modes + 1,)),
            *two(SLICES, cores), *two(SLICES, modes), *two(SLICES, depth), *two(SLICES, depth),
            *two(SLICES, modes), *two(SLICES, modes, cores),
            *two(cores), *two(depth), *two(modes), *two(modes, cores),
            *two(len(SCATTER), modes),
        ],
        compiler_params=pltpu.CompilerParams(
            collective_id=0, has_side_effects=True, vmem_limit_bytes=48 * 1024 * 1024
        ),
        name="truncate",
    )(unfolded, pltpu.with_memory_space_constraint(start_block, pltpu.HBM))


def emit_kernel(*refs):
    count = len(refs) // 2
    sem = refs[-1]
    copies = [pltpu.make_async_copy(refs[k], refs[count + k], sem.at[k]) for k in range(count)]
    for copy in copies:
        copy.start()
    for copy in copies:
        copy.wait()


def emit(*arrays):
    count = len(arrays)
    return pl.pallas_call(
        emit_kernel,
        out_shape=tuple(jax.ShapeDtypeStruct(x.shape, x.dtype) for x in arrays),
        in_specs=[pl.BlockSpec(memory_space=pl.ANY)] * count,
        out_specs=(pl.BlockSpec(memory_space=pltpu.HBM),) * count,
        scratch_shapes=[pltpu.SemaphoreType.DMA((count,))],
        compiler_params=pltpu.CompilerParams(vmem_limit_bytes=1024 * 1024),
        name="emit",
    )(*arrays)


def per_device(unfolded, start_block):
    return emit(*program(unfolded, start_block, lax.axis_size("mode"), lax.axis_size("rest")))


def solution(mesh):
    return jax.shard_map(
        per_device,
        mesh=mesh,
        in_specs=(P("mode", "rest"), P()),
        out_specs=(P(), P(), P("mode", "rest")),
        check_vma=False,
    )
```
